256 devices in a mesh: tile: 32 (over x_lo, z, core), head: 8 (over y, x_hi).
Axes of the slice: x: 4 (x_hi: 2, x_lo: 2; x = x_hi * 2 + x_lo), y: 4, z: 8, core: 2. Of those that a mesh axis runs over, the one named last changes fastest.
Arguments:
- attn_proj: bfloat16 [32, 3, 192, 3, 3072], P('tile', None, 'head')
- mlp_proj: bfloat16 [32, 3, 192, 6144], P('tile', None, 'head'), may hold values from -6 to 6
- stream: bfloat16 [32, 3, 192, 3072], P('tile', None, 'head'), may hold values from -6 to 6
- text_len: int32 [32], P('tile'), may hold values from 1 to 192, as said below
- q_gain: float32 [128], replicated
- k_gain: float32 [128], replicated
- w_out_attn: bfloat16 [3072, 3072], P('head', 'tile'), may hold values from -0.0625 to 0.0625
- w_out_mlp: bfloat16 [6144, 3072], P('head', 'tile'), may hold values from -0.0625 to 0.0625
- bias_out: float32 [3072], replicated, may hold values from -3 to 3
- gate_mod: float32 [32, 3072], P('tile'), may hold values from -4 to 4
- final_shift: float32 [32, 3072], P('tile'), may hold values from -3 to 3
- final_scale: float32 [32, 3072], P('tile'), may hold values from -3 to 3
- w_final: bfloat16 [3072, 64], replicated, may hold values from -0.109375 to 0.109375
- b_final: float32 [64], replicated, may hold values from -3 to 3
- latent: float32 [32, 2, 192, 64], P('tile', None, 'head'), may hold values from -6 to 6
- step_size: float32 [32], P('tile'), may hold values from -0.4 to -0.1
Outputs:
- hidden_out: bfloat16 [32, 3, 192, 3072], P('tile', None, 'head')
- latent_next: float32 [32, 2, 192, 64], P('tile', None, 'head')
The draws below stay inside these ranges and needn't reach their ends.
Inputs may be any that keep to these rules, and one draw needn't show every extreme that they name: `text_len`: live text slots of each request; some request has all 192 text slots live in every draw.
All inputs are finite; a program needn't handle non-finite values.
Results may differ from the reference program's by a relative error of at most 0.0098.
Values may be sent and summed in bfloat16 or wider, within the bound.
A program may use at most 128 MiB of HBM per device.

```python
import math
import jax
import jax.numpy as jnp
from jax import lax

D = 3072
HEADS = 24
HEAD_DIM = 128
CHANNELS = 64
FFW = 6144
SLOTS = 192
GRID_W = 32
REQUESTS = 32


def draw_attn_proj(key, part):
    shape = (REQUESTS, 3, SLOTS, 3, D)
    first_key = jax.random.fold_in(key, 11)
    base = jax.random.normal(first_key, shape, jnp.float32)
    return base.astype(jnp.bfloat16)


def draw_gain_common(key, salt):
    gain_key = jax.random.fold_in(key, salt)
    values = jax.random.uniform(gain_key, (HEAD_DIM,), jnp.float32, 0.6, 1.8)
    return values


def draw_q_gain(key, part):
    return draw_gain_common(key, 21)


def draw_k_gain(key, part):
    return draw_gain_common(key, 22)


def draw_text_len(key, part):
    length_key = jax.random.fold_in(key, 31)
    which_key = jax.random.fold_in(key, 32)
    lengths = jax.random.randint(length_key, (REQUESTS,), 1, SLOTS + 1)
    which = jax.random.randint(which_key, (), 0, REQUESTS)
    return jnp.where(jnp.arange(REQUESTS) == which, SLOTS, lengths).astype(jnp.int32)


def level_of(rng, extent, shards, smallest, high):
    factor_of = 1.0
    for position, blocks in shards:
        heights = jax.random.uniform(jax.random.fold_in(jax.random.fold_in(rng, 6), position), (blocks,), jnp.float32, smallest / len(shards), high / len(shards))
        factor_of = factor_of * jnp.repeat(jnp.exp(heights), extent[position] // blocks).reshape((-1,) + (1,) * (len(extent) - 1 - position))
    return factor_of


def centred(own_key, dims, width, limit, cuts=(), kind=jnp.bfloat16):
    level = level_of(own_key, dims, cuts, -0.22, 0.18) if cuts else 1.0
    values = jax.random.normal(own_key, dims, jnp.float32) * width * level
    return jnp.minimum(jnp.maximum(values, -limit), limit).astype(kind)


def setup_inputs(seed: int = 0) -> dict:
    seeds = jax.random.split(jax.random.key(seed), 17)
    return {
        "attn_proj": draw_attn_proj(jax.random.fold_in(seeds[16], 71), 0),
        "mlp_proj": centred(seeds[1], (REQUESTS, 3, SLOTS, FFW), 1.0, 6.0, ((0, 32), (2, 8))),
        "stream": centred(seeds[2], (REQUESTS, 3, SLOTS, D), 1.0, 6.0, ((0, 32), (2, 8))),
        "text_len": draw_text_len(jax.random.fold_in(seeds[16], 71), 0),
        "q_gain": draw_q_gain(jax.random.fold_in(seeds[16], 71), 0),
        "k_gain": draw_k_gain(jax.random.fold_in(seeds[16], 71), 0),
        "w_out_attn": centred(seeds[6], (D, D), (D + FFW) ** -0.5, 0.0625, ((0, 8), (1, 32))),
        "w_out_mlp": centred(seeds[7], (FFW, D), (D + FFW) ** -0.5, 0.0625, ((0, 8), (1, 32))),
        "bias_out": centred(seeds[8], (D,), 0.5, 3.0, (), jnp.float32),
        "gate_mod": centred(seeds[9], (REQUESTS, D), 1.0, 4.0, ((0, 32),), jnp.float32),
        "final_shift": centred(seeds[10], (REQUESTS, D), 0.5, 3.0, ((0, 32),), jnp.float32),
        "final_scale": centred(seeds[11], (REQUESTS, D), 0.5, 3.0, ((0, 32),), jnp.float32),
        "w_final": centred(seeds[12], (D, CHANNELS), D ** -0.5, 0.109375),
        "b_final": centred(seeds[13], (CHANNELS,), 0.5, 3.0, (), jnp.float32),
        "latent": centred(seeds[14], (REQUESTS, 2, SLOTS, CHANNELS), 1.0, 6.0, ((0, 32), (2, 8)), jnp.float32),
        "step_size": jnp.clip(-0.4 + 0.3 * jax.random.uniform(seeds[15], (REQUESTS,), jnp.float32) ** level_of(seeds[15], (REQUESTS,), ((0, 32),), -0.2, 0.2), -0.4, -0.1),
    }


def rope_tables(positions):
    pairs_zero = HEAD_DIM // 16
    pairs_axis = (HEAD_DIM // 2 - pairs_zero) // 2
    freqs = 10000.0 ** (-jnp.arange(pairs_axis, dtype=jnp.float32) / pairs_axis)
    count = positions.shape[0]
    angles = [jnp.zeros((count, HEAD_DIM // 2), jnp.float32)]
    for block in range(1, 3):
        image_index = (block - 1) * SLOTS + positions
        rows = (image_index // GRID_W).astype(jnp.float32)
        columns = (image_index % GRID_W).astype(jnp.float32)
        angles.append(jnp.concatenate([jnp.zeros((count, pairs_zero), jnp.float32), rows[:, None] * freqs[None, :], columns[:, None] * freqs[None, :]], axis=1))
    stacked = jnp.stack(angles)
    return (jnp.cos(stacked), jnp.sin(stacked))

def prepare(raw, gain, cosine, sine):
    normed = raw * lax.rsqrt(lax.optimization_barrier(jnp.mean(raw * raw, axis=-1, keepdims=True)) + 1e-06) * gain
    halves = normed.reshape(normed.shape[:-1] + (HEAD_DIM // 2, 2))
    first = halves[..., 0]
    second = halves[..., 1]
    cosine = cosine[None, :, :, None, :]
    sine = sine[None, :, :, None, :]
    rotated = jnp.stack([first * cosine - second * sine, first * sine + second * cosine], axis=-1)
    return rotated.reshape(raw.shape).astype(jnp.bfloat16)

def attend_request(inputs):
    queries, keys, values, live = inputs
    scores = jnp.einsum('qhd,khd->hqk', queries.astype(jnp.float32), keys.astype(jnp.float32)) / math.sqrt(HEAD_DIM)
    scores = jnp.where(live[None, None, :], scores, -jnp.inf)
    top = lax.optimization_barrier(jnp.max(scores, axis=-1, keepdims=True))
    weights = jnp.exp(scores - top)
    total = lax.optimization_barrier(jnp.sum(weights, axis=-1))
    mixed = jnp.einsum('hqk,khd->qhd', weights.astype(jnp.bfloat16).astype(jnp.float32), values.astype(jnp.float32))
    return (mixed / jnp.transpose(total)[:, :, None]).astype(jnp.bfloat16)

def reference(attn_proj, mlp_proj, stream, text_len, q_gain, k_gain, w_out_attn, w_out_mlp, bias_out, gate_mod, final_shift, final_scale, w_final, b_final, latent, step_size):
    positions = jnp.arange(SLOTS, dtype=jnp.int32)
    cosine, sine = rope_tables(positions)
    head_shape = (REQUESTS, 3, SLOTS, HEADS, HEAD_DIM)
    queries = prepare(attn_proj[:, :, :, 0].astype(jnp.float32).reshape(head_shape), q_gain, cosine, sine)
    keys = prepare(attn_proj[:, :, :, 1].astype(jnp.float32).reshape(head_shape), k_gain, cosine, sine)
    values = attn_proj[:, :, :, 2].reshape(head_shape)
    text_live = positions[None, :] < text_len[:, None]
    image_live = jnp.ones_like(text_live)
    live = jnp.stack([text_live, image_live, image_live], axis=1).reshape(REQUESTS, 3 * SLOTS)
    flat_shape = (REQUESTS, 3 * SLOTS, HEADS, HEAD_DIM)
    attn_out = lax.map(attend_request, (queries.reshape(flat_shape), keys.reshape(flat_shape), values.reshape(flat_shape), live))
    attn_out = attn_out.reshape(REQUESTS * 3 * SLOTS, D)
    mlp_act = jax.nn.gelu(mlp_proj.astype(jnp.float32), approximate=True).astype(jnp.bfloat16)
    proj = jnp.dot(attn_out, w_out_attn, preferred_element_type=jnp.float32) + jnp.dot(mlp_act.reshape(REQUESTS * 3 * SLOTS, FFW), w_out_mlp, preferred_element_type=jnp.float32)
    proj = proj.reshape(REQUESTS, 3, SLOTS, D)
    updated = stream.astype(jnp.float32) + gate_mod[:, None, None, :] * (proj + bias_out)
    hidden_out = updated.astype(jnp.bfloat16)
    image = updated[:, 1:]
    center = image - lax.optimization_barrier(jnp.mean(image, axis=-1, keepdims=True))
    variance = lax.optimization_barrier(jnp.mean(center * center, axis=-1, keepdims=True))
    normed = center * lax.rsqrt(variance + 1e-06)
    modulated = ((1.0 + final_scale[:, None, None, :]) * normed + final_shift[:, None, None, :]).astype(jnp.bfloat16)
    velocity = jnp.dot(modulated.reshape(REQUESTS * 2 * SLOTS, D), w_final, preferred_element_type=jnp.float32).reshape(REQUESTS, 2, SLOTS, CHANNELS) + b_final
    latent_next = latent + step_size[:, None, None, None] * velocity
    return (hidden_out, latent_next)
```

```python
import functools
import math

import jax
import jax.numpy as jnp
import numpy as np
from jax import lax
from jax.experimental import pallas as pl
from jax.experimental.pallas import tpu as pltpu
from jax.sharding import PartitionSpec as P

HEAD_DIM = 128
SLOTS = 192
GRID_W = 32
MESH = pl.DeviceIdType.MESH
F32 = jnp.float32
BF16 = jnp.bfloat16


def rope_constants(groups):
    zero = HEAD_DIM // 16
    axis = (HEAD_DIM // 2 - zero) // 2
    own = SLOTS // groups
    freqs = (10000.0 ** (-np.arange(axis, dtype=np.float32) / np.float32(axis))).astype(np.float32)
    angles = np.zeros((3, SLOTS, HEAD_DIM // 2), np.float32)
    for block in (1, 2):
        index = (block - 1) * SLOTS + np.arange(SLOTS)
        angles[block, :, zero : zero + axis] = (index // GRID_W).astype(np.float32)[:, None] * freqs
        angles[block, :, zero + axis :] = (index % GRID_W).astype(np.float32)[:, None] * freqs
    order = angles.reshape(3, groups, own, HEAD_DIM // 2).transpose(1, 0, 2, 3)
    wide = np.repeat(order.astype(np.float64), 2, axis=-1)
    sign = np.where(np.arange(HEAD_DIM) % 2 == 0, -1.0, 1.0)
    cosine = np.cos(wide).astype(np.float32)
    sine = (np.sin(wide) * sign).astype(np.float32)
    slot = np.full((3, SLOTS), -1, np.int32)
    slot[0] = np.arange(SLOTS)
    slot = slot.reshape(3, groups, own).transpose(1, 0, 2).reshape(1, -1)
    return cosine, sine, slot


def swap_pairs(x, even):
    return jnp.where(even, pltpu.roll(x, HEAD_DIM - 1, axis=x.ndim - 1), pltpu.roll(x, 1, axis=x.ndim - 1))


def layer_kernel(
    cfg,
    text_len,
    step_size,
    attn_in,
    mlp_in,
    stream_in,
    weight_attn,
    weight_mlp,
    w_final,
    cosine,
    sine,
    slot_number,
    q_gain,
    k_gain,
    bias_out,
    gate,
    shift,
    scale,
    b_final,
    latent,
    hidden_out,
    latent_out,
    got_attn,
    got_mlp,
    weights,
    queries,
    keys,
    values,
    mlp_act,
    act,
    product,
    outgoing,
    incoming,
    mine,
    updated,
    stream,
    final_w,
    table_c,
    table_s,
    local_sem,
    attn_send,
    attn_recv,
    mlp_send,
    mlp_recv,
    ring_send,
    ring_recv,
    side_send,
    side_recv,
    part_send,
    part_recv,
):
    heads_n, z_n, chunks, own_rows, own_slots = cfg
    tile = lax.axis_index("tile")
    head = lax.axis_index("head")
    core = tile % 2
    depth = (tile // 2) % z_n
    half = tile // (2 * z_n)
    width = got_attn.shape[4]
    units = got_mlp.shape[3]
    local_heads = width // HEAD_DIM
    shard = weights.shape[1]
    per_chunk = weights.shape[0] // chunks
    columns = shard * per_chunk
    rows = heads_n * own_rows

    def tile_at(half_, depth_, core_):
        return half_ * (2 * z_n) + depth_ * 2 + core_

    up = tile_at(half, (depth + 1) % z_n, core)
    down = tile_at(half, (depth + z_n - 1) % z_n, core)
    across = tile_at(1 - half, depth, core)
    sibling = tile_at(half, depth, 1 - core)

    def local_copies():
        at = pl.ds(pl.multiple_of(head * width, width), width)
        mt = pl.ds(pl.multiple_of(head * units, units), units)
        return [
            pltpu.make_async_copy(attn_in.at[:, :, :, at], got_attn.at[head], local_sem.at[0]),
            pltpu.make_async_copy(mlp_in.at[:, :, mt], got_mlp.at[head], local_sem.at[1]),
            pltpu.make_async_copy(weight_attn, weights.at[tile, :, pl.ds(0, width)], local_sem.at[2]),
            pltpu.make_async_copy(weight_mlp, weights.at[tile, :, pl.ds(width, units)], local_sem.at[3]),
            pltpu.make_async_copy(stream_in, stream, local_sem.at[4]),
            pltpu.make_async_copy(w_final, final_w, local_sem.at[5]),
        ]

    for copy in local_copies():
        copy.start()

    barrier = pltpu.get_barrier_semaphore()
    for neighbour in (up, down, across, sibling):
        pl.semaphore_signal(barrier, inc=1, device_id={"tile": neighbour}, device_id_type=MESH)

    def greet(i, _):
        pl.semaphore_signal(barrier, inc=1, device_id={"head": (head + i) % heads_n}, device_id_type=MESH)
        return 0

    lax.fori_loop(1, heads_n, greet, 0)
    pl.semaphore_wait(barrier, heads_n - 1 + 4)

    def attn_copy(i, peer, source):
        return pltpu.make_async_remote_copy(
            src_ref=attn_in.at[:, :, :, pl.ds(pl.multiple_of(peer * width, width), width)],
            dst_ref=got_attn.at[source],
            send_sem=attn_send.at[i],
            recv_sem=attn_recv.at[i],
            device_id={"head": peer},
            device_id_type=MESH,
        )

    def mlp_copy(i, peer, source):
        return pltpu.make_async_remote_copy(
            src_ref=mlp_in.at[:, :, pl.ds(pl.multiple_of(peer * units, units), units)],
            dst_ref=got_mlp.at[source],
            send_sem=mlp_send.at[i],
            recv_sem=mlp_recv.at[i],
            device_id={"head": peer},
            device_id_type=MESH,
        )

    def send_attn(i, _):
        attn_copy(i, (head + i) % heads_n, head).start()
        return 0

    def send_mlp(i, _):
        mlp_copy(i, (head + i) % heads_n, head).start()
        return 0

    lax.fori_loop(1, heads_n, send_attn, 0)

    def ring_copy(stream_, direction, step, slot):
        return pltpu.make_async_remote_copy(
            src_ref=weights.at[slot],
            dst_ref=weights.at[slot],
            send_sem=ring_send.at[stream_, direction, step],
            recv_sem=ring_recv.at[stream_, direction, step],
            device_id={"tile": up if direction == 0 else down},
            device_id_type=MESH,
        )

    def side_copy(index, slot, to):
        return pltpu.make_async_remote_copy(
            src_ref=weights.at[slot],
            dst_ref=weights.at[slot],
            send_sem=side_send.at[index],
            recv_sem=side_recv.at[index],
            device_id={"tile": to},
            device_id_type=MESH,
        )

    reach = (z_n // 2, z_n - 1 - z_n // 2)

    def half_of(stream_):
        return half if stream_ == 0 else 1 - half

    def arrival(stream_, direction, step):
        offset = z_n - step if direction == 0 else step
        slot = tile_at(half_of(stream_), (depth + offset) % z_n, core)
        return slot, stream_ * z_n + (offset if offset < z_n else 0)

    def begin(stream_):
        slot = tile_at(half_of(stream_), depth, core)
        ring_copy(stream_, 0, 1, slot).start()
        ring_copy(stream_, 1, 1, slot).start()
        side_copy(stream_ * z_n, slot, sibling).start()

    def advance(stream_, step):
        for direction in (0, 1):
            if step <= reach[direction]:
                slot, number = arrival(stream_, direction, step)
                ring_copy(stream_, direction, step, slot).wait_recv()
                if step < reach[direction]:
                    ring_copy(stream_, direction, step + 1, slot).start()
                side_copy(number, slot, sibling).start()

    cross = 2 * z_n
    locals_ = local_copies()
    locals_[2].wait()
    locals_[3].wait()
    side_copy(cross, tile, across).start()
    begin(0)
    lax.fori_loop(1, heads_n, send_mlp, 0)

    even = lax.broadcasted_iota(jnp.int32, (own_slots, HEAD_DIM), 1) % 2 == 0
    even8 = even[:8]
    for j, gain_ref in enumerate((q_gain, k_gain)):
        gain = jnp.broadcast_to(gain_ref[...], (8, HEAD_DIM))
        swapped = swap_pairs(gain, even8)[0:1]
        table_c[j] = cosine[...] * gain_ref[...]
        table_s[j] = sine[...] * swapped

    def prepare(group):
        for block in range(3):
            where = pl.ds(pl.multiple_of(group * own_rows + block * own_slots, 8), own_slots)
            for j, target in enumerate((queries, keys)):
                raw = got_attn[group, block, j].astype(F32)
                for n in range(local_heads):
                    x = raw[:, n * HEAD_DIM : (n + 1) * HEAD_DIM]
                    r = lax.rsqrt(jnp.mean(x * x, axis=-1, keepdims=True) + 1e-06)
                    y = r * (x * table_c[j, where] + swap_pairs(x, even) * table_s[j, where])
                    target[n, where] = y
            raw = got_attn[group, block, 2].astype(F32)
            for n in range(local_heads):
                values[n, where] = raw[:, n * HEAD_DIM : (n + 1) * HEAD_DIM]

    def receive_attn(i, _):
        source = (head + heads_n - i) % heads_n
        attn_copy(i, head, source).wait_recv()
        prepare(source)
        return 0

    def activate(group):
        for block in range(3):
            where = pl.ds(pl.multiple_of(group * own_rows + block * own_slots, 8), own_slots)
            x = got_mlp[group, block].astype(F32)
            inner = math.sqrt(2.0 / math.pi) * (x + 0.044715 * (x * x * x))
            mlp_act[where] = 0.5 * x * (1.0 + jnp.tanh(inner))

    def receive_mlp(i, _):
        source = (head + heads_n - i) % heads_n
        mlp_copy(i, head, source).wait_recv()
        activate(source)
        return 0

    live = slot_number[...] < text_len[0]
    factor = math.log2(math.e) / math.sqrt(HEAD_DIM)
    band = rows // 3

    def attend(n):
        k = keys[n].astype(BF16)
        v = values[n].astype(BF16)
        for part in range(3):
            q = queries[n, pl.ds(part * band, band)].astype(BF16)
            scores = lax.dot_general(q, k, (((1,), (1,)), ((), ())), preferred_element_type=F32)
            scores = jnp.where(live, scores, -1e30)
            top = jnp.max(scores, axis=-1, keepdims=True)
            weight = jnp.exp2((scores - top) * factor)
            total = jnp.sum(weight, axis=-1, keepdims=True)
            mixed = jnp.dot(weight.astype(BF16), v, preferred_element_type=F32)
            act[pl.ds(part * band, band), n * HEAD_DIM : (n + 1) * HEAD_DIM] = (mixed / total).astype(BF16)

    locals_[0].wait()
    prepare(head)
    side_copy(cross, across, across).wait_recv()
    begin(1)
    lax.fori_loop(1, heads_n // 2, receive_attn, 0)
    advance(0, 1)
    advance(1, 1)
    lax.fori_loop(heads_n // 2, heads_n, receive_attn, 0)
    advance(0, 2)
    advance(1, 2)
    for n in range(local_heads):
        attend(n)
        if n == 1:
            advance(0, 3)
            advance(1, 3)
    locals_[1].wait()
    activate(head)
    lax.fori_loop(1, heads_n, receive_mlp, 0)
    act[:, width:] = mlp_act[...].astype(BF16)
    advance(0, 4)
    advance(1, 4)
    for stream_ in (0, 1):
        for offset in range(z_n):
            slot = tile_at(half_of(stream_), (depth + offset) % z_n, 1 - core)
            side_copy(stream_ * z_n + offset, slot, sibling).wait_recv()

    def part_copy(chunk, i, peer, source):
        return pltpu.make_async_remote_copy(
            src_ref=outgoing.at[chunk, peer],
            dst_ref=incoming.at[chunk, source],
            send_sem=part_send.at[chunk, i],
            recv_sem=part_recv.at[chunk, i],
            device_id={"head": peer},
            device_id_type=MESH,
        )

    def project(chunk, _):
        block = weights[pl.ds(chunk * per_chunk, per_chunk)].reshape(columns, width + units)
        product[...] = lax.dot_general(
            act[...], block, (((1,), (1,)), ((), ())), preferred_element_type=F32
        )

        def send_part(i, _):
            peer = (head + i) % heads_n
            part = product[pl.ds(pl.multiple_of(peer * own_rows, 8), own_rows)]
            outgoing[chunk, peer] = part.astype(BF16)
            part_copy(chunk, i, peer, head).start()
            return 0

        lax.fori_loop(1, heads_n, send_part, 0)
        mine[chunk] = product[pl.ds(pl.multiple_of(head * own_rows, 8), own_rows)]
        return 0

    lax.fori_loop(0, chunks, project, 0)

    locals_[4].wait()
    locals_[5].wait()

    def collect(chunk, _):
        at = pl.ds(pl.multiple_of(chunk * columns, 128), columns)

        def wait_part(i, _):
            part_copy(chunk, i, head, (head + heads_n - i) % heads_n).wait_recv()
            return 0

        lax.fori_loop(1, heads_n, wait_part, 0)
        total = mine[chunk]
        for i in range(1, heads_n):
            total = total + incoming[chunk, (head + i) % heads_n].astype(F32)
        for block in range(3):
            part = slice(block * own_slots, (block + 1) * own_slots)
            new = stream[block, :, at].astype(F32) + gate[:, at] * (total[part] + bias_out[:, at])
            updated[block, :, at] = new
            hidden_out[block, :, at] = new.astype(BF16)
        return 0

    lax.fori_loop(0, chunks, collect, 0)

    for block in (1, 2):
        image = updated[block]
        center = image - jnp.mean(image, axis=-1, keepdims=True)
        variance = jnp.mean(center * center, axis=-1, keepdims=True)
        normed = center * lax.rsqrt(variance + 1e-06)
        modulated = ((1.0 + scale[...]) * normed + shift[...]).astype(BF16)
        velocity = lax.dot_general(
            modulated, final_w[...], (((1,), (1,)), ((), ())), preferred_element_type=F32
        )
        latent_out[block - 1] = latent[block - 1] + step_size[0] * (velocity + b_final[...])

    def drain(i, _):
        attn_copy(i, (head + i) % heads_n, head).wait_send()
        mlp_copy(i, (head + i) % heads_n, head).wait_send()
        return 0

    lax.fori_loop(1, heads_n, drain, 0)

    def drain_parts(chunk, _):
        def one(i, _):
            part_copy(chunk, i, (head + i) % heads_n, head).wait_send()
            return 0

        lax.fori_loop(1, heads_n, one, 0)
        return 0

    lax.fori_loop(0, chunks, drain_parts, 0)
    side_copy(cross, tile, across).wait_send()
    for stream_ in (0, 1):
        for offset in range(z_n):
            slot = tile_at(half_of(stream_), (depth + offset) % z_n, core)
            side_copy(stream_ * z_n + offset, slot, sibling).wait_send()
        for direction in (0, 1):
            for step in range(1, reach[direction] + 1):
                offset = z_n - step + 1 if direction == 0 else step - 1
                slot = tile_at(half_of(stream_), (depth + offset) % z_n, core)
                ring_copy(stream_, direction, step, slot).wait_send()


def solution(mesh):
    heads_n = mesh.shape["head"]
    tiles_n = mesh.shape["tile"]
    z_n = tiles_n // 4
    chunks = 8
    cosine, sine, slot_number = rope_constants(heads_n)

    def per_device(
        attn_proj,
        mlp_proj,
        stream,
        text_len,
        q_gain,
        k_gain,
        w_out_attn,
        w_out_mlp,
        bias_out,
        gate_mod,
        final_shift,
        final_scale,
        w_final,
        b_final,
        latent,
        step_size,
    ):
        own_slots = attn_proj.shape[2]
        own_rows = 3 * own_slots
        rows = heads_n * own_rows
        features = attn_proj.shape[4]
        width, shard = w_out_attn.shape
        units = w_out_mlp.shape[0]
        local_heads = width // HEAD_DIM
        columns = features // chunks
        channels = w_final.shape[1]
        cfg = (heads_n, z_n, chunks, own_rows, own_slots)
        any_ = pl.BlockSpec(memory_space=pl.ANY)
        vmem = pl.BlockSpec(memory_space=pltpu.VMEM)
        smem = pl.BlockSpec(memory_space=pltpu.SMEM)
        dma = pltpu.SemaphoreType.DMA
        hidden, latent_next = pl.pallas_call(
            functools.partial(layer_kernel, cfg),
            out_shape=(
                jax.ShapeDtypeStruct((3, own_slots, features), BF16),
                jax.ShapeDtypeStruct((2, own_slots, channels), F32),
            ),
            in_specs=[smem, smem] + [any_] * 6 + [vmem] * 11,
            out_specs=(vmem, vmem),
            scratch_shapes=[
                pltpu.VMEM((heads_n, 3, 3, own_slots, width), BF16),
                pltpu.VMEM((heads_n, 3, own_slots, units), BF16),
                pltpu.VMEM((tiles_n, shard, width + units), BF16),
                pltpu.VMEM((local_heads, rows, HEAD_DIM), F32),
                pltpu.VMEM((local_heads, rows, HEAD_DIM), F32),
                pltpu.VMEM((local_heads, rows, HEAD_DIM), F32),
                pltpu.VMEM((rows, units), F32),
                pltpu.VMEM((rows, width + units), BF16),
                pltpu.VMEM((rows, columns), F32),
                pltpu.VMEM((chunks, heads_n, own_rows, columns), BF16),
                pltpu.VMEM((chunks, heads_n, own_rows, columns), BF16),
                pltpu.VMEM((chunks, own_rows, columns), F32),
                pltpu.VMEM((3, own_slots, features), F32),
                pltpu.VMEM((3, own_slots, features), BF16),
                pltpu.VMEM((channels, features), BF16),
                pltpu.VMEM((2, rows, HEAD_DIM), F32),
                pltpu.VMEM((2, rows, HEAD_DIM), F32),
                dma((6,)),
                dma((heads_n,)),
                dma((heads_n,)),
                dma((heads_n,)),
                dma((heads_n,)),
                dma((2, 2, z_n)),
                dma((2, 2, z_n)),
                dma((2 * z_n + 1,)),
                dma((2 * z_n + 1,)),
                dma((chunks, heads_n)),
                dma((chunks, heads_n)),
            ],
            compiler_params=pltpu.CompilerParams(
                collective_id=0, has_side_effects=True, vmem_limit_bytes=56 * 1024 * 1024
            ),
        )(
            text_len,
            step_size,
            jnp.transpose(attn_proj[0], (0, 2, 1, 3)),
            mlp_proj[0],
            stream[0],
            w_out_attn.T,
            w_out_mlp.T,
            w_final.T,
            jnp.asarray(cosine.reshape(rows, HEAD_DIM)),
            jnp.asarray(sine.reshape(rows, HEAD_DIM)),
            jnp.asarray(slot_number),
            q_gain[None],
            k_gain[None],
            bias_out[None],
            gate_mod,
            final_shift,
            final_scale,
            b_final[None],
            latent[0],
        )
        return hidden[None], latent_next[None]

    placed = (
        P("tile", None, "head", None, None),
        P("tile", None, "head", None),
        P("tile", None, "head", None),
        P("tile"),
        P(),
        P(),
        P("head", "tile"),
        P("head", "tile"),
        P(),
        P("tile", None),
        P("tile", None),
        P("tile", None),
        P(),
        P(),
        P("tile", None, "head", None),
        P("tile"),
    )
    return jax.shard_map(
        per_device,
        mesh=mesh,
        in_specs=placed,
        out_specs=(P("tile", None, "head", None), P("tile", None, "head", None)),
        check_vma=False,
    )
```

```python
import functools
import math

import jax
import jax.numpy as jnp
import numpy as np
from jax import lax
from jax.experimental import pallas as pl
from jax.experimental.pallas import tpu as pltpu
from jax.sharding import PartitionSpec as P

HEAD_DIM = 128
SLOTS = 192
GRID_W = 32
MESH = pl.DeviceIdType.MESH
F32 = jnp.float32
BF16 = jnp.bfloat16


def rope_constants(groups):
    zero = HEAD_DIM // 16
    axis = (HEAD_DIM // 2 - zero) // 2
    own = SLOTS // groups
    freqs = (10000.0 ** (-np.arange(axis, dtype=np.float32) / np.float32(axis))).astype(np.float32)
    angles = np.zeros((3, SLOTS, HEAD_DIM // 2), np.float32)
    for block in (1, 2):
        index = (block - 1) * SLOTS + np.arange(SLOTS)
        angles[block, :, zero : zero + axis] = (index // GRID_W).astype(np.float32)[:, None] * freqs
        angles[block, :, zero + axis :] = (index % GRID_W).astype(np.float32)[:, None] * freqs
    order = angles.reshape(3, groups, own, HEAD_DIM // 2).transpose(1, 0, 2, 3)
    wide = np.repeat(order.astype(np.float64), 2, axis=-1)
    sign = np.where(np.arange(HEAD_DIM) % 2 == 0, -1.0, 1.0)
    cosine = np.cos(wide).astype(np.float32)
    sine = (np.sin(wide) * sign).astype(np.float32)
    slot = np.full((3, SLOTS), -1, np.int32)
    slot[0] = np.arange(SLOTS)
    slot = slot.reshape(3, groups, own).transpose(1, 0, 2).reshape(1, -1)
    return cosine, sine, slot


def swap_pairs(x, even):
    return jnp.where(even, pltpu.roll(x, HEAD_DIM - 1, axis=x.ndim - 1), pltpu.roll(x, 1, axis=x.ndim - 1))


def layer_kernel(
    cfg,
    text_len,
    step_size,
    attn_in,
    mlp_in,
    stream_in,
    weight_attn,
    weight_mlp,
    w_final,
    cosine,
    sine,
    slot_number,
    q_gain,
    k_gain,
    bias_out,
    gate,
    shift,
    scale,
    b_final,
    latent,
    hidden_out,
    latent_out,
    got_attn,
    got_mlp,
    weights,
    queries,
    keys,
    values,
    mlp_act,
    act,
    product,
    y_out,
    y_in,
    y_pass,
    y_got,
    x_out,
    x_in,
    x_pass,
    x_got,
    mine,
    updated,
    stream,
    final_w,
    table_c,
    table_s,
    local_sem,
    attn_send,
    attn_recv,
    mlp_send,
    mlp_recv,
    ring_send,
    ring_recv,
    side_send,
    side_recv,
    y_send,
    y_recv,
    y_pass_send,
    y_pass_recv,
    x_send,
    x_recv,
    x_pass_send,
    x_pass_recv,
):
    heads_n, z_n, pairs, own_rows, own_slots = cfg
    y_n = heads_n // 2
    tile = lax.axis_index("tile")
    head = lax.axis_index("head")
    core = tile % 2
    depth = (tile // 2) % z_n
    half = tile // (2 * z_n)
    row_y = head // 2
    side_x = head % 2
    width = got_attn.shape[4]
    units = got_mlp.shape[3]
    local_heads = width // HEAD_DIM
    shard = weights.shape[1]
    per_chunk = weights.shape[0] // (2 * pairs)
    columns = shard * per_chunk
    rows = heads_n * own_rows

    def tile_at(half_, depth_, core_):
        return half_ * (2 * z_n) + depth_ * 2 + core_

    up = tile_at(half, (depth + 1) % z_n, core)
    down = tile_at(half, (depth + z_n - 1) % z_n, core)
    across = tile_at(1 - half, depth, core)
    sibling = tile_at(half, depth, 1 - core)

    def head_at(dy, dx):
        return ((row_y + dy + y_n) % y_n) * 2 + (side_x + dx) % 2

    def peer_of(i):
        return head_at(i // 2, i % 2)

    def source_of(i):
        return head_at(-(i // 2), i % 2)

    def local_copies():
        at = pl.ds(pl.multiple_of(head * width, width), width)
        mt = pl.ds(pl.multiple_of(head * units, units), units)
        return [
            pltpu.make_async_copy(attn_in.at[:, :, :, at], got_attn.at[head], local_sem.at[0]),
            pltpu.make_async_copy(mlp_in.at[:, :, mt], got_mlp.at[head], local_sem.at[1]),
            pltpu.make_async_copy(weight_attn, weights.at[tile, :, pl.ds(0, width)], local_sem.at[2]),
            pltpu.make_async_copy(weight_mlp, weights.at[tile, :, pl.ds(width, units)], local_sem.at[3]),
            pltpu.make_async_copy(stream_in, stream, local_sem.at[4]),
            pltpu.make_async_copy(w_final, final_w, local_sem.at[5]),
        ]

    for copy in local_copies():
        copy.start()

    barrier = pltpu.get_barrier_semaphore()
    for neighbour in (up, down, across, sibling):
        pl.semaphore_signal(barrier, inc=1, device_id={"tile": neighbour}, device_id_type=MESH)

    def greet(i, _):
        pl.semaphore_signal(barrier, inc=1, device_id={"head": peer_of(i)}, device_id_type=MESH)
        return 0

    lax.fori_loop(1, heads_n, greet, 0)
    pl.semaphore_wait(barrier, heads_n - 1 + 4)

    def attn_copy(i, peer, source):
        return pltpu.make_async_remote_copy(
            src_ref=attn_in.at[:, :, :, pl.ds(pl.multiple_of(peer * width, width), width)],
            dst_ref=got_attn.at[source],
            send_sem=attn_send.at[i],
            recv_sem=attn_recv.at[i],
            device_id={"head": peer},
            device_id_type=MESH,
        )

    def mlp_copy(i, peer, source):
        return pltpu.make_async_remote_copy(
            src_ref=mlp_in.at[:, :, pl.ds(pl.multiple_of(peer * units, units), units)],
            dst_ref=got_mlp.at[source],
            send_sem=mlp_send.at[i],
            recv_sem=mlp_recv.at[i],
            device_id={"head": peer},
            device_id_type=MESH,
        )

    def send_attn(i, _):
        attn_copy(i, peer_of(i), head).start()
        return 0

    def send_mlp(i, _):
        mlp_copy(i, peer_of(i), head).start()
        return 0

    def ring_copy(stream_, direction, step, slot):
        return pltpu.make_async_remote_copy(
            src_ref=weights.at[slot],
            dst_ref=weights.at[slot],
            send_sem=ring_send.at[stream_, direction, step],
            recv_sem=ring_recv.at[stream_, direction, step],
            device_id={"tile": up if direction == 0 else down},
            device_id_type=MESH,
        )

    def side_copy(index, slot, to):
        return pltpu.make_async_remote_copy(
            src_ref=weights.at[slot],
            dst_ref=weights.at[slot],
            send_sem=side_send.at[index],
            recv_sem=side_recv.at[index],
            device_id={"tile": to},
            device_id_type=MESH,
        )

    far, near = z_n // 2, z_n - 1 - z_n // 2
    reach = ((far, near), (near, far))

    def half_of(stream_):
        return half if stream_ == 0 else 1 - half

    def arrival(stream_, direction, step):
        offset = z_n - step if direction == 0 else step
        slot = tile_at(half_of(stream_), (depth + offset) % z_n, core)
        return slot, stream_ * z_n + (offset if offset < z_n else 0)

    def begin(stream_):
        slot = tile_at(half_of(stream_), depth, core)
        ring_copy(stream_, 0, 1, slot).start()
        ring_copy(stream_, 1, 1, slot).start()
        side_copy(stream_ * z_n, slot, sibling).start()

    def advance(stream_, step):
        for direction in (0, 1):
            if step <= reach[stream_][direction]:
                slot, number = arrival(stream_, direction, step)
                ring_copy(stream_, direction, step, slot).wait_recv()
                if step < reach[stream_][direction]:
                    ring_copy(stream_, direction, step + 1, slot).start()
                side_copy(number, slot, sibling).start()

    cross = 2 * z_n
    locals_ = local_copies()
    locals_[2].wait()
    locals_[3].wait()
    side_copy(cross, tile, across).start()
    begin(0)
    lax.fori_loop(1, heads_n, send_attn, 0)
    lax.fori_loop(1, heads_n, send_mlp, 0)

    even = lax.broadcasted_iota(jnp.int32, (own_slots, HEAD_DIM), 1) % 2 == 0
    even8 = even[:8]
    for j, gain_ref in enumerate((q_gain, k_gain)):
        gain = jnp.broadcast_to(gain_ref[...], (8, HEAD_DIM))
        swapped = swap_pairs(gain, even8)[0:1]
        table_c[j] = cosine[...] * gain_ref[...]
        table_s[j] = sine[...] * swapped

    def prepare(group):
        for block in range(3):
            where = pl.ds(pl.multiple_of(group * own_rows + block * own_slots, 8), own_slots)
            for j, target in enumerate((queries, keys)):
                raw = got_attn[group, block, j].astype(F32)
                for n in range(local_heads):
                    x = raw[:, n * HEAD_DIM : (n + 1) * HEAD_DIM]
                    r = lax.rsqrt(jnp.mean(x * x, axis=-1, keepdims=True) + 1e-06)
                    y = r * (x * table_c[j, where] + swap_pairs(x, even) * table_s[j, where])
                    target[n, where] = y
            raw = got_attn[group, block, 2].astype(F32)
            for n in range(local_heads):
                values[n, where] = raw[:, n * HEAD_DIM : (n + 1) * HEAD_DIM]

    def receive_attn(i, _):
        source = source_of(i)
        attn_copy(i, head, source).wait_recv()
        prepare(source)
        return 0

    def activate(group):
        for block in range(3):
            where = pl.ds(pl.multiple_of(group * own_rows + block * own_slots, 8), own_slots)
            x = got_mlp[group, block].astype(F32)
            inner = math.sqrt(2.0 / math.pi) * (x + 0.044715 * (x * x * x))
            mlp_act[where] = 0.5 * x * (1.0 + jnp.tanh(inner))

    def receive_mlp(i, _):
        source = source_of(i)
        mlp_copy(i, head, source).wait_recv()
        activate(source)
        return 0

    live = slot_number[...] < text_len[0]
    factor = math.log2(math.e) / math.sqrt(HEAD_DIM)
    band = rows // 3

    def attend(n):
        k = keys[n].astype(BF16)
        v = values[n].astype(BF16)
        for part in range(3):
            q = queries[n, pl.ds(part * band, band)].astype(BF16)
            scores = lax.dot_general(q, k, (((1,), (1,)), ((), ())), preferred_element_type=F32)
            scores = jnp.where(live, scores, -1e30)
            top = jnp.max(scores, axis=-1, keepdims=True)
            weight = jnp.exp2((scores - top) * factor)
            total = jnp.sum(weight, axis=-1, keepdims=True)
            mixed = jnp.dot(weight.astype(BF16), v, preferred_element_type=F32)
            act[pl.ds(part * band, band), n * HEAD_DIM : (n + 1) * HEAD_DIM] = (mixed / total).astype(BF16)

    locals_[0].wait()
    prepare(head)
    side_copy(cross, across, across).wait_recv()
    begin(1)
    lax.fori_loop(1, heads_n // 2, receive_attn, 0)
    advance(0, 1)
    advance(1, 1)
    lax.fori_loop(heads_n // 2, heads_n, receive_attn, 0)
    advance(0, 2)
    advance(1, 2)
    for n in range(local_heads):
        attend(n)
    locals_[1].wait()
    activate(head)
    lax.fori_loop(1, heads_n, receive_mlp, 0)
    act[:, width:] = mlp_act[...].astype(BF16)
    locals_[4].wait()
    locals_[5].wait()

    def wait_sibling(offsets):
        for stream_ in (0, 1):
            for offset in offsets:
                slot = tile_at(half_of(stream_), (depth + offset) % z_n, 1 - core)
                side_copy(stream_ * z_n + offset, slot, sibling).wait_recv()

    def y_copy(p, dy, peer_y):
        return pltpu.make_async_remote_copy(
            src_ref=y_out.at[p, peer_y],
            dst_ref=y_in.at[p, dy],
            send_sem=y_send.at[p, dy],
            recv_sem=y_recv.at[p, dy],
            device_id={"head": peer_y * 2 + side_x},
            device_id_type=MESH,
        )

    def y_pass_copy(p):
        return pltpu.make_async_remote_copy(
            src_ref=y_pass.at[p],
            dst_ref=y_got.at[p],
            send_sem=y_pass_send.at[p],
            recv_sem=y_pass_recv.at[p],
            device_id={"head": head_at(0, 1)},
            device_id_type=MESH,
        )

    def x_copy(p):
        return pltpu.make_async_remote_copy(
            src_ref=x_out.at[p],
            dst_ref=x_in.at[p],
            send_sem=x_send.at[p],
            recv_sem=x_recv.at[p],
            device_id={"head": head_at(0, 1)},
            device_id_type=MESH,
        )

    def x_pass_copy(p, dy):
        return pltpu.make_async_remote_copy(
            src_ref=x_pass.at[p, dy],
            dst_ref=x_got.at[p, dy],
            send_sem=x_pass_send.at[p, dy],
            recv_sem=x_pass_recv.at[p, dy],
            device_id={"head": head_at(dy, 0)},
            device_id_type=MESH,
        )

    def group_rows(kind, p, group):
        return product[kind, p, pl.ds(pl.multiple_of(group * own_rows, 8), own_rows)]

    def chunk_of(kind, p):
        order = p + (p // 2) * (1 - 2 * (p % 2))
        return kind * pairs + (depth // 2 + order) % pairs

    def pass_on(p):
        for dy in range(1, y_n):
            y_copy(p, dy, row_y).wait_recv()
        for dx in (0, 1):
            side = (side_x + dx) % 2
            total = group_rows(0, p, row_y * 2 + side)
            for dy in range(1, y_n):
                total = total + y_in[p, dy, side].astype(F32)
            if dx == 0:
                mine[0, p] = total
            else:
                y_pass[p] = total.astype(BF16)
        y_pass_copy(p).start()
        x_copy(p).wait_recv()
        for dy in range(1, y_n):
            peer_y = (row_y + dy) % y_n
            total = group_rows(1, p, peer_y * 2 + side_x) + x_in[p, peer_y].astype(F32)
            x_pass[p, dy] = total.astype(BF16)
            x_pass_copy(p, dy).start()
        mine[1, p] = group_rows(1, p, head) + x_in[p, row_y].astype(F32)

    wait_sibling([0] + [o for o in (1, z_n - 1) if o != 0])

    def project(k, _):
        p, kind = k // 2, k % 2

        @pl.when(k == 2)
        def _():
            for step in range(3, far):
                advance(0, step)
                advance(1, step)
            wait_sibling([o for o in range(2, z_n - 1) if o != far])

        @pl.when(k == 2 * pairs - 2)
        def _():
            pass_on(0)
            advance(0, far)
            advance(1, far)
            wait_sibling([far])

        block = weights[pl.ds(chunk_of(kind, p) * per_chunk, per_chunk)].reshape(columns, width + units)
        product[kind, p] = lax.dot_general(
            act[...], block, (((1,), (1,)), ((), ())), preferred_element_type=F32
        )

        @pl.when(kind == 0)
        def _():
            for dy in range(1, y_n):
                peer_y = (row_y + dy) % y_n
                for side in (0, 1):
                    y_out[p, peer_y, side] = group_rows(0, p, peer_y * 2 + side).astype(BF16)
                y_copy(p, dy, peer_y).start()

        @pl.when(kind == 1)
        def _():
            for peer_y in range(y_n):
                x_out[p, peer_y] = group_rows(1, p, peer_y * 2 + 1 - side_x).astype(BF16)
            x_copy(p).start()

        return 0

    lax.fori_loop(0, 2 * pairs, project, 0)

    def store(kind, p, total):
        at = pl.ds(pl.multiple_of(chunk_of(kind, p) * columns, 128), columns)
        for block in range(3):
            part = slice(block * own_slots, (block + 1) * own_slots)
            new = stream[block, :, at].astype(F32) + gate[:, at] * (total[part] + bias_out[:, at])
            updated[block, :, at] = new
            hidden_out[block, :, at] = new.astype(BF16)

    def collect(p):
        y_pass_copy(p).wait_recv()
        store(0, p, mine[0, p] + y_got[p].astype(F32))
        total = mine[1, p]
        for dy in range(1, y_n):
            x_pass_copy(p, dy).wait_recv()
            total = total + x_got[p, dy].astype(F32)
        store(1, p, total)

    def finish(p, _):
        @pl.when(p < pairs)
        def _():
            pass_on(p)

        collect(p - 1)
        return 0

    lax.fori_loop(1, pairs + 1, finish, 0)

    for block in (1, 2):
        image = updated[block]
        center = image - jnp.mean(image, axis=-1, keepdims=True)
        variance = jnp.mean(center * center, axis=-1, keepdims=True)
        normed = center * lax.rsqrt(variance + 1e-06)
        modulated = ((1.0 + scale[...]) * normed + shift[...]).astype(BF16)
        velocity = lax.dot_general(
            modulated, final_w[...], (((1,), (1,)), ((), ())), preferred_element_type=F32
        )
        latent_out[block - 1] = latent[block - 1] + step_size[0] * (velocity + b_final[...])

    def drain(i, _):
        attn_copy(i, peer_of(i), head).wait_send()
        mlp_copy(i, peer_of(i), head).wait_send()
        return 0

    lax.fori_loop(1, heads_n, drain, 0)

    def drain_parts(p, _):
        for dy in range(1, y_n):
            y_copy(p, dy, (row_y + dy) % y_n).wait_send()
            x_pass_copy(p, dy).wait_send()
        y_pass_copy(p).wait_send()
        x_copy(p).wait_send()
        return 0

    lax.fori_loop(0, pairs, drain_parts, 0)
    side_copy(cross, tile, across).wait_send()
    for stream_ in (0, 1):
        for offset in range(z_n):
            slot = tile_at(half_of(stream_), (depth + offset) % z_n, core)
            side_copy(stream_ * z_n + offset, slot, sibling).wait_send()
        for direction in (0, 1):
            for step in range(1, reach[stream_][direction] + 1):
                offset = z_n - step + 1 if direction == 0 else step - 1
                slot = tile_at(half_of(stream_), (depth + offset) % z_n, core)
                ring_copy(stream_, direction, step, slot).wait_send()


def solution(mesh):
    heads_n = mesh.shape["head"]
    tiles_n = mesh.shape["tile"]
    z_n = tiles_n // 4
    pairs = 4
    cosine, sine, slot_number = rope_constants(heads_n)

    def per_device(
        attn_proj,
        mlp_proj,
        stream,
        text_len,
        q_gain,
        k_gain,
        w_out_attn,
        w_out_mlp,
        bias_out,
        gate_mod,
        final_shift,
        final_scale,
        w_final,
        b_final,
        latent,
        step_size,
    ):
        own_slots = attn_proj.shape[2]
        own_rows = 3 * own_slots
        rows = heads_n * own_rows
        features = attn_proj.shape[4]
        width, shard = w_out_attn.shape
        units = w_out_mlp.shape[0]
        local_heads = width // HEAD_DIM
        columns = features // (2 * pairs)
        y_n = heads_n // 2
        channels = w_final.shape[1]
        cfg = (heads_n, z_n, pairs, own_rows, own_slots)
        any_ = pl.BlockSpec(memory_space=pl.ANY)
        vmem = pl.BlockSpec(memory_space=pltpu.VMEM)
        smem = pl.BlockSpec(memory_space=pltpu.SMEM)
        dma = pltpu.SemaphoreType.DMA
        hidden, latent_next = pl.pallas_call(
            functools.partial(layer_kernel, cfg),
            out_shape=(
                jax.ShapeDtypeStruct((3, own_slots, features), BF16),
                jax.ShapeDtypeStruct((2, own_slots, channels), F32),
            ),
            in_specs=[smem, smem] + [any_] * 6 + [vmem] * 11,
            out_specs=(vmem, vmem),
            scratch_shapes=[
                pltpu.VMEM((heads_n, 3, 3, own_slots, width), BF16),
                pltpu.VMEM((heads_n, 3, own_slots, units), BF16),
                pltpu.VMEM((tiles_n, shard, width + units), BF16),
                pltpu.VMEM((local_heads, rows, HEAD_DIM), F32),
                pltpu.VMEM((local_heads, rows, HEAD_DIM), F32),
                pltpu.VMEM((local_heads, rows, HEAD_DIM), F32),
                pltpu.VMEM((rows, units), F32),
                pltpu.VMEM((rows, width + units), BF16),
                pltpu.VMEM((2, pairs, rows, columns), F32),
                pltpu.VMEM((pairs, y_n, 2, own_rows, columns), BF16),
                pltpu.VMEM((pairs, y_n, 2, own_rows, columns), BF16),
                pltpu.VMEM((pairs, own_rows, columns), BF16),
                pltpu.VMEM((pairs, own_rows, columns), BF16),
                pltpu.VMEM((pairs, y_n, own_rows, columns), BF16),
                pltpu.VMEM((pairs, y_n, own_rows, columns), BF16),
                pltpu.VMEM((pairs, y_n, own_rows, columns), BF16),
                pltpu.VMEM((pairs, y_n, own_rows, columns), BF16),
                pltpu.VMEM((2, pairs, own_rows, columns), F32),
                pltpu.VMEM((3, own_slots, features), F32),
                pltpu.VMEM((3, own_slots, features), BF16),
                pltpu.VMEM((channels, features), BF16),
                pltpu.VMEM((2, rows, HEAD_DIM), F32),
                pltpu.VMEM((2, rows, HEAD_DIM), F32),
                dma((6,)),
                dma((heads_n,)),
                dma((heads_n,)),
                dma((heads_n,)),
                dma((heads_n,)),
                dma((2, 2, z_n)),
                dma((2, 2, z_n)),
                dma((2 * z_n + 1,)),
                dma((2 * z_n + 1,)),
                dma((pairs, y_n)),
                dma((pairs, y_n)),
                dma((pairs,)),
                dma((pairs,)),
                dma((pairs,)),
                dma((pairs,)),
                dma((pairs, y_n)),
                dma((pairs, y_n)),
            ],
            compiler_params=pltpu.CompilerParams(
                collective_id=0, has_side_effects=True, vmem_limit_bytes=56 * 1024 * 1024
            ),
        )(
            text_len,
            step_size,
            jnp.transpose(attn_proj[0], (0, 2, 1, 3)),
            mlp_proj[0],
            stream[0],
            w_out_attn.T,
            w_out_mlp.T,
            w_final.T,
            jnp.asarray(cosine.reshape(rows, HEAD_DIM)),
            jnp.asarray(sine.reshape(rows, HEAD_DIM)),
            jnp.asarray(slot_number),
            q_gain[None],
            k_gain[None],
            bias_out[None],
            gate_mod,
            final_shift,
            final_scale,
            b_final[None],
            latent[0],
        )
        return hidden[None], latent_next[None]

    placed = (
        P("tile", None, "head", None, None),
        P("tile", None, "head", None),
        P("tile", None, "head", None),
        P("tile"),
        P(),
        P(),
        P("head", "tile"),
        P("head", "tile"),
        P(),
        P("tile", None),
        P("tile", None),
        P("tile", None),
        P(),
        P(),
        P("tile", None, "head", None),
        P("tile"),
    )
    return jax.shard_map(
        per_device,
        mesh=mesh,
        in_specs=placed,
        out_specs=(P("tile", None, "head", None), P("tile", None, "head", None)),
        check_vma=False,
    )
```

```python
import functools
import math

import jax
import jax.numpy as jnp
import numpy as np
from jax import lax
from jax.experimental import pallas as pl
from jax.experimental.pallas import tpu as pltpu
from jax.sharding import PartitionSpec as P

HEAD_DIM = 128
SLOTS = 192
GRID_W = 32
MESH = pl.DeviceIdType.MESH
F32 = jnp.float32
BF16 = jnp.bfloat16


def rope_constants(groups):
    zero = HEAD_DIM // 16
    axis = (HEAD_DIM // 2 - zero) // 2
    own = SLOTS // groups
    freqs = (10000.0 ** (-np.arange(axis, dtype=np.float32) / np.float32(axis))).astype(np.float32)
    angles = np.zeros((3, SLOTS, HEAD_DIM // 2), np.float32)
    for block in (1, 2):
        index = (block - 1) * SLOTS + np.arange(SLOTS)
        angles[block, :, zero : zero + axis] = (index // GRID_W).astype(np.float32)[:, None] * freqs
        angles[block, :, zero + axis :] = (index % GRID_W).astype(np.float32)[:, None] * freqs
    order = angles.reshape(3, groups, own, HEAD_DIM // 2).transpose(1, 0, 2, 3)
    wide = np.repeat(order.astype(np.float64), 2, axis=-1)
    sign = np.where(np.arange(HEAD_DIM) % 2 == 0, -1.0, 1.0)
    cosine = np.cos(wide).astype(np.float32)
    sine = (np.sin(wide) * sign).astype(np.float32)
    slot = np.full((3, SLOTS), -1, np.int32)
    slot[0] = np.arange(SLOTS)
    slot = slot.reshape(3, groups, own).transpose(1, 0, 2).reshape(1, -1)
    return cosine, sine, slot


def swap_pairs(x, even):
    return jnp.where(even, pltpu.roll(x, HEAD_DIM - 1, axis=x.ndim - 1), pltpu.roll(x, 1, axis=x.ndim - 1))


def layer_kernel(
    cfg,
    text_len,
    step_size,
    attn_in,
    mlp_in,
    stream_in,
    weight_attn,
    weight_mlp,
    w_final,
    cosine,
    sine,
    slot_number,
    q_gain,
    k_gain,
    bias_out,
    gate,
    shift,
    scale,
    b_final,
    latent,
    hidden_out,
    latent_out,
    got_attn,
    got_mlp,
    weights,
    queries,
    keys,
    values,
    mlp_act,
    act,
    product,
    y_out,
    y_in,
    y_pass,
    y_got,
    x_out,
    x_in,
    x_pass,
    x_got,
    mine,
    updated,
    stream,
    final_w,
    table_c,
    table_s,
    local_sem,
    attn_send,
    attn_recv,
    mlp_send,
    mlp_recv,
    ring_send,
    ring_recv,
    side_send,
    side_recv,
    y_send,
    y_recv,
    y_pass_send,
    y_pass_recv,
    x_send,
    x_recv,
    x_pass_send,
    x_pass_recv,
):
    heads_n, z_n, pairs, own_rows, own_slots = cfg
    y_n = heads_n // 2
    tile = lax.axis_index("tile")
    head = lax.axis_index("head")
    core = tile % 2
    depth = (tile // 2) % z_n
    half = tile // (2 * z_n)
    row_y = head // 2
    side_x = head % 2
    width = got_attn.shape[4]
    units = got_mlp.shape[3]
    local_heads = width // HEAD_DIM
    shard = weights.shape[1]
    columns = shard * 4
    rows = heads_n * own_rows

    def tile_at(half_, depth_, core_):
        return half_ * (2 * z_n) + depth_ * 2 + core_

    def shard_at(half_, depth_, core_):
        return depth_ * 4 + half_ * 2 + core_

    own_shard = shard_at(half, depth, core)
    up = tile_at(half, (depth + 1) % z_n, core)
    down = tile_at(half, (depth + z_n - 1) % z_n, core)
    across = tile_at(1 - half, depth, core)
    sibling = tile_at(half, depth, 1 - core)

    def head_at(dy, dx):
        return ((row_y + dy + y_n) % y_n) * 2 + (side_x + dx) % 2

    def peer_of(i):
        return head_at(i // 2, i % 2)

    def source_of(i):
        return head_at(-(i // 2), i % 2)

    def local_copies():
        at = pl.ds(pl.multiple_of(head * width, width), width)
        mt = pl.ds(pl.multiple_of(head * units, units), units)
        return [
            pltpu.make_async_copy(attn_in.at[:, :, :, at], got_attn.at[head], local_sem.at[0]),
            pltpu.make_async_copy(mlp_in.at[:, :, mt], got_mlp.at[head], local_sem.at[1]),
            pltpu.make_async_copy(weight_attn, weights.at[own_shard, :, pl.ds(0, width)], local_sem.at[2]),
            pltpu.make_async_copy(weight_mlp, weights.at[own_shard, :, pl.ds(width, units)], local_sem.at[3]),
            pltpu.make_async_copy(stream_in, stream, local_sem.at[4]),
            pltpu.make_async_copy(w_final, final_w, local_sem.at[5]),
        ]

    for copy in local_copies():
        copy.start()

    barrier = pltpu.get_barrier_semaphore()
    for neighbour in (up, down, across, sibling):
        pl.semaphore_signal(barrier, inc=1, device_id={"tile": neighbour}, device_id_type=MESH)

    def greet(i, _):
        pl.semaphore_signal(barrier, inc=1, device_id={"head": peer_of(i)}, device_id_type=MESH)
        return 0

    lax.fori_loop(1, heads_n, greet, 0)
    pl.semaphore_wait(barrier, heads_n - 1 + 4)

    def attn_copy(i, peer, source):
        return pltpu.make_async_remote_copy(
            src_ref=attn_in.at[:, :, :, pl.ds(pl.multiple_of(peer * width, width), width)],
            dst_ref=got_attn.at[source],
            send_sem=attn_send.at[i],
            recv_sem=attn_recv.at[i],
            device_id={"head": peer},
            device_id_type=MESH,
        )

    def mlp_copy(i, peer, source):
        return pltpu.make_async_remote_copy(
            src_ref=mlp_in.at[:, :, pl.ds(pl.multiple_of(peer * units, units), units)],
            dst_ref=got_mlp.at[source],
            send_sem=mlp_send.at[i],
            recv_sem=mlp_recv.at[i],
            device_id={"head": peer},
            device_id_type=MESH,
        )

    def send_attn(i, _):
        attn_copy(i, peer_of(i), head).start()
        return 0

    def send_mlp(i, _):
        mlp_copy(i, peer_of(i), head).start()
        return 0

    def ring_copy(stream_, direction, step, slot):
        return pltpu.make_async_remote_copy(
            src_ref=weights.at[slot],
            dst_ref=weights.at[slot],
            send_sem=ring_send.at[stream_, direction, step],
            recv_sem=ring_recv.at[stream_, direction, step],
            device_id={"tile": up if direction == 0 else down},
            device_id_type=MESH,
        )

    def side_copy(index, slot, to):
        return pltpu.make_async_remote_copy(
            src_ref=weights.at[slot],
            dst_ref=weights.at[slot],
            send_sem=side_send.at[index],
            recv_sem=side_recv.at[index],
            device_id={"tile": to},
            device_id_type=MESH,
        )

    far, near = z_n // 2, z_n - 1 - z_n // 2
    reach = ((far, near), (near, far))

    def half_of(stream_):
        return half if stream_ == 0 else 1 - half

    def arrival(stream_, direction, step):
        offset = z_n - step if direction == 0 else step
        slot = shard_at(half_of(stream_), (depth + offset) % z_n, core)
        return slot, stream_ * z_n + (offset if offset < z_n else 0)

    def begin(stream_):
        slot = shard_at(half_of(stream_), depth, core)
        ring_copy(stream_, 0, 1, slot).start()
        ring_copy(stream_, 1, 1, slot).start()
        side_copy(stream_ * z_n, slot, sibling).start()

    def advance(stream_, step):
        for direction in (0, 1):
            if step <= reach[stream_][direction]:
                slot, number = arrival(stream_, direction, step)
                ring_copy(stream_, direction, step, slot).wait_recv()
                if step < reach[stream_][direction]:
                    ring_copy(stream_, direction, step + 1, slot).start()
                side_copy(number, slot, sibling).start()

    cross = 2 * z_n
    locals_ = local_copies()
    locals_[2].wait()
    locals_[3].wait()
    side_copy(cross, own_shard, across).start()
    begin(0)
    lax.fori_loop(1, heads_n, send_attn, 0)
    lax.fori_loop(1, heads_n, send_mlp, 0)

    even = lax.broadcasted_iota(jnp.int32, (own_slots, HEAD_DIM), 1) % 2 == 0
    even8 = even[:8]
    for j, gain_ref in enumerate((q_gain, k_gain)):
        gain = jnp.broadcast_to(gain_ref[...], (8, HEAD_DIM))
        swapped = swap_pairs(gain, even8)[0:1]
        table_c[j] = cosine[...] * gain_ref[...]
        table_s[j] = sine[...] * swapped

    def prepare(group):
        for block in range(3):
            where = pl.ds(pl.multiple_of(group * own_rows + block * own_slots, 8), own_slots)
            for j, target in enumerate((queries, keys)):
                raw = got_attn[group, block, j].astype(F32)
                for n in range(local_heads):
                    x = raw[:, n * HEAD_DIM : (n + 1) * HEAD_DIM]
                    r = lax.rsqrt(jnp.mean(x * x, axis=-1, keepdims=True) + 1e-06)
                    y = r * (x * table_c[j, where] + swap_pairs(x, even) * table_s[j, where])
                    target[n, where] = y
            raw = got_attn[group, block, 2].astype(F32)
            for n in range(local_heads):
                values[n, where] = raw[:, n * HEAD_DIM : (n + 1) * HEAD_DIM]

    def receive_attn(i, _):
        source = source_of(i)
        attn_copy(i, head, source).wait_recv()
        prepare(source)
        return 0

    def activate(group):
        for block in range(3):
            where = pl.ds(pl.multiple_of(group * own_rows + block * own_slots, 8), own_slots)
            x = got_mlp[group, block].astype(F32)
            inner = math.sqrt(2.0 / math.pi) * (x + 0.044715 * (x * x * x))
            mlp_act[where] = 0.5 * x * (1.0 + jnp.tanh(inner))

    def receive_mlp(i, _):
        source = source_of(i)
        mlp_copy(i, head, source).wait_recv()
        activate(source)
        return 0

    live = slot_number[...] < text_len[0]
    factor = math.log2(math.e) / math.sqrt(HEAD_DIM)
    band = rows // 3

    def attend(n):
        k = keys[n].astype(BF16)
        v = values[n].astype(BF16)
        for part in range(3):
            q = queries[n, pl.ds(part * band, band)].astype(BF16)
            scores = lax.dot_general(q, k, (((1,), (1,)), ((), ())), preferred_element_type=F32)
            scores = jnp.where(live, scores, -1e30)
            top = jnp.max(scores, axis=-1, keepdims=True)
            weight = jnp.exp2((scores - top) * factor)
            total = jnp.sum(weight, axis=-1, keepdims=True)
            mixed = jnp.dot(weight.astype(BF16), v, preferred_element_type=F32)
            act[pl.ds(part * band, band), n * HEAD_DIM : (n + 1) * HEAD_DIM] = (mixed / total).astype(BF16)

    locals_[0].wait()
    prepare(head)
    side_copy(cross, shard_at(1 - half, depth, core), across).wait_recv()
    begin(1)
    advance(0, 1)
    advance(1, 1)
    lax.fori_loop(1, heads_n // 2, receive_attn, 0)
    lax.fori_loop(heads_n // 2, heads_n, receive_attn, 0)
    advance(0, 2)
    advance(1, 2)
    for n in range(local_heads):
        attend(n)
    locals_[1].wait()
    activate(head)
    lax.fori_loop(1, heads_n, receive_mlp, 0)
    act[:, width:] = mlp_act[...].astype(BF16)
    locals_[4].wait()
    locals_[5].wait()

    def wait_sibling(offsets):
        for stream_ in (0, 1):
            for offset in offsets:
                slot = shard_at(half_of(stream_), (depth + offset) % z_n, 1 - core)
                side_copy(stream_ * z_n + offset, slot, sibling).wait_recv()

    def y_copy(p, dy, peer_y):
        return pltpu.make_async_remote_copy(
            src_ref=y_out.at[p, peer_y],
            dst_ref=y_in.at[p, dy],
            send_sem=y_send.at[p, dy],
            recv_sem=y_recv.at[p, dy],
            device_id={"head": peer_y * 2 + side_x},
            device_id_type=MESH,
        )

    def y_pass_copy(p):
        return pltpu.make_async_remote_copy(
            src_ref=y_pass.at[p],
            dst_ref=y_got.at[p],
            send_sem=y_pass_send.at[p],
            recv_sem=y_pass_recv.at[p],
            device_id={"head": head_at(0, 1)},
            device_id_type=MESH,
        )

    def x_copy(p):
        return pltpu.make_async_remote_copy(
            src_ref=x_out.at[p],
            dst_ref=x_in.at[p],
            send_sem=x_send.at[p],
            recv_sem=x_recv.at[p],
            device_id={"head": head_at(0, 1)},
            device_id_type=MESH,
        )

    def x_pass_copy(p, dy):
        return pltpu.make_async_remote_copy(
            src_ref=x_pass.at[p, dy],
            dst_ref=x_got.at[p, dy],
            send_sem=x_pass_send.at[p, dy],
            recv_sem=x_pass_recv.at[p, dy],
            device_id={"head": head_at(dy, 0)},
            device_id_type=MESH,
        )

    def group_rows(kind, p, group):
        return product[kind, p, pl.ds(pl.multiple_of(group * own_rows, 8), own_rows)]

    def offset_of(kind, p):
        return p + 1 if kind == 1 else (z_n - p) % z_n

    def pass_on(p):
        for dy in range(1, y_n):
            y_copy(p, dy, row_y).wait_recv()
        for dx in (0, 1):
            side = (side_x + dx) % 2
            total = group_rows(0, p, row_y * 2 + side)
            for dy in range(1, y_n):
                total = total + y_in[p, dy, side].astype(F32)
            if dx == 0:
                mine[0, p] = total
            else:
                y_pass[p] = total.astype(BF16)
        y_pass_copy(p).start()
        x_copy(p).wait_recv()
        for dy in range(1, y_n):
            peer_y = (row_y + dy) % y_n
            total = group_rows(1, p, peer_y * 2 + side_x) + x_in[p, peer_y].astype(F32)
            x_pass[p, dy] = total.astype(BF16)
            x_pass_copy(p, dy).start()
        mine[1, p] = group_rows(1, p, head) + x_in[p, row_y].astype(F32)

    wait_sibling([offset_of(kind, 0) for kind in (0, 1)])

    def project(k, _):
        p, kind = k // 2, k % 2

        @pl.when(k == 2)
        def _():
            wait_sibling([offset_of(kind, 1) for kind in (0, 1)])
            for step in range(3, far):
                advance(0, step)
                advance(1, step)

        @pl.when(k == 4)
        def _():
            wait_sibling([offset_of(kind, p) for p in range(2, pairs - 1) for kind in (0, 1)])

        @pl.when(k == 2 * pairs - 2)
        def _():
            pass_on(0)
            advance(0, far)
            advance(1, far)
            wait_sibling([offset_of(kind, pairs - 1) for kind in (0, 1)])

        offset = kind * (p + 1) + (1 - kind) * ((z_n - p) % z_n)
        nearest = (depth + offset) % z_n
        block = weights[pl.ds(nearest * 4, 4)].reshape(columns, width + units)
        product[kind, p] = lax.dot_general(
            act[...], block, (((1,), (1,)), ((), ())), preferred_element_type=F32
        )

        @pl.when(kind == 0)
        def _():
            for dy in range(1, y_n):
                peer_y = (row_y + dy) % y_n
                for side in (0, 1):
                    y_out[p, peer_y, side] = group_rows(0, p, peer_y * 2 + side).astype(BF16)
                y_copy(p, dy, peer_y).start()

        @pl.when(kind == 1)
        def _():
            for peer_y in range(y_n):
                x_out[p, peer_y] = group_rows(1, p, peer_y * 2 + 1 - side_x).astype(BF16)
            x_copy(p).start()

        return 0

    lax.fori_loop(0, 2 * pairs, project, 0)

    def collect(p):
        y_pass_copy(p).wait_recv()
        mine[0, p] = mine[0, p] + y_got[p].astype(F32)
        total = mine[1, p]
        for dy in range(1, y_n):
            x_pass_copy(p, dy).wait_recv()
            total = total + x_got[p, dy].astype(F32)
        mine[1, p] = total

    def finish(p, _):
        @pl.when(p < pairs)
        def _():
            pass_on(p)

        collect(p - 1)
        return 0

    lax.fori_loop(1, pairs + 1, finish, 0)

    def sum_at(z):
        offset = (z + z_n - depth) % z_n
        kind = (offset + z_n - 1) % z_n // pairs
        p = (1 - kind) * (offset - 1) + kind * ((z_n - offset) % z_n)
        return mine[1 - kind, p]

    narrow = columns // 2
    for pair in range(z_n // 2):
        low, high = sum_at(2 * pair), sum_at(2 * pair + 1)
        for side in (0, 1):
            piece = slice(side * narrow, (side + 1) * narrow)
            total = jnp.concatenate([low[:, piece], high[:, piece]], axis=-1)
            start = side * narrow * z_n + pair * columns
            at = slice(start, start + columns)
            for block in range(3):
                part = slice(block * own_slots, (block + 1) * own_slots)
                new = stream[block, :, at].astype(F32) + gate[:, at] * (total[part] + bias_out[:, at])
                updated[block, :, at] = new
                hidden_out[block, :, at] = new.astype(BF16)

    for block in (1, 2):
        image = updated[block]
        center = image - jnp.mean(image, axis=-1, keepdims=True)
        variance = jnp.mean(center * center, axis=-1, keepdims=True)
        normed = center * lax.rsqrt(variance + 1e-06)
        modulated = ((1.0 + scale[...]) * normed + shift[...]).astype(BF16)
        velocity = lax.dot_general(
            modulated, final_w[...], (((1,), (1,)), ((), ())), preferred_element_type=F32
        )
        latent_out[block - 1] = latent[block - 1] + step_size[0] * (velocity + b_final[...])

    def drain(i, _):
        attn_copy(i, peer_of(i), head).wait_send()
        mlp_copy(i, peer_of(i), head).wait_send()
        return 0

    lax.fori_loop(1, heads_n, drain, 0)

    def drain_parts(p, _):
        for dy in range(1, y_n):
            y_copy(p, dy, (row_y + dy) % y_n).wait_send()
            x_pass_copy(p, dy).wait_send()
        y_pass_copy(p).wait_send()
        x_copy(p).wait_send()
        return 0

    lax.fori_loop(0, pairs, drain_parts, 0)
    side_copy(cross, own_shard, across).wait_send()
    for stream_ in (0, 1):
        for offset in range(z_n):
            slot = shard_at(half_of(stream_), (depth + offset) % z_n, core)
            side_copy(stream_ * z_n + offset, slot, sibling).wait_send()
        for direction in (0, 1):
            for step in range(1, reach[stream_][direction] + 1):
                offset = z_n - step + 1 if direction == 0 else step - 1
                slot = shard_at(half_of(stream_), (depth + offset) % z_n, core)
                ring_copy(stream_, direction, step, slot).wait_send()


def solution(mesh):
    heads_n = mesh.shape["head"]
    tiles_n = mesh.shape["tile"]
    z_n = tiles_n // 4
    pairs = 4
    cosine, sine, slot_number = rope_constants(heads_n)

    def per_device(
        attn_proj,
        mlp_proj,
        stream,
        text_len,
        q_gain,
        k_gain,
        w_out_attn,
        w_out_mlp,
        bias_out,
        gate_mod,
        final_shift,
        final_scale,
        w_final,
        b_final,
        latent,
        step_size,
    ):
        own_slots = attn_proj.shape[2]
        own_rows = 3 * own_slots
        rows = heads_n * own_rows
        features = attn_proj.shape[4]
        width, shard = w_out_attn.shape
        units = w_out_mlp.shape[0]
        local_heads = width // HEAD_DIM
        columns = features // (2 * pairs)
        y_n = heads_n // 2
        channels = w_final.shape[1]
        cfg = (heads_n, z_n, pairs, own_rows, own_slots)
        any_ = pl.BlockSpec(memory_space=pl.ANY)
        vmem = pl.BlockSpec(memory_space=pltpu.VMEM)
        smem = pl.BlockSpec(memory_space=pltpu.SMEM)
        dma = pltpu.SemaphoreType.DMA
        hidden, latent_next = pl.pallas_call(
            functools.partial(layer_kernel, cfg),
            out_shape=(
                jax.ShapeDtypeStruct((3, own_slots, features), BF16),
                jax.ShapeDtypeStruct((2, own_slots, channels), F32),
            ),
            in_specs=[smem, smem] + [any_] * 6 + [vmem] * 11,
            out_specs=(vmem, vmem),
            scratch_shapes=[
                pltpu.VMEM((heads_n, 3, 3, own_slots, width), BF16),
                pltpu.VMEM((heads_n, 3, own_slots, units), BF16),
                pltpu.VMEM((tiles_n, shard, width + units), BF16),
                pltpu.VMEM((local_heads, rows, HEAD_DIM), F32),
                pltpu.VMEM((local_heads, rows, HEAD_DIM), F32),
                pltpu.VMEM((local_heads, rows, HEAD_DIM), F32),
                pltpu.VMEM((rows, units), F32),
                pltpu.VMEM((rows, width + units), BF16),
                pltpu.VMEM((2, pairs, rows, columns), F32),
                pltpu.VMEM((pairs, y_n, 2, own_rows, columns), BF16),
                pltpu.VMEM((pairs, y_n, 2, own_rows, columns), BF16),
                pltpu.VMEM((pairs, own_rows, columns), BF16),
                pltpu.VMEM((pairs, own_rows, columns), BF16),
                pltpu.VMEM((pairs, y_n, own_rows, columns), BF16),
                pltpu.VMEM((pairs, y_n, own_rows, columns), BF16),
                pltpu.VMEM((pairs, y_n, own_rows, columns), BF16),
                pltpu.VMEM((pairs, y_n, own_rows, columns), BF16),
                pltpu.VMEM((2, pairs, own_rows, columns), F32),
                pltpu.VMEM((3, own_slots, features), F32),
                pltpu.VMEM((3, own_slots, features), BF16),
                pltpu.VMEM((channels, features), BF16),
                pltpu.VMEM((2, rows, HEAD_DIM), F32),
                pltpu.VMEM((2, rows, HEAD_DIM), F32),
                dma((6,)),
                dma((heads_n,)),
                dma((heads_n,)),
                dma((heads_n,)),
                dma((heads_n,)),
                dma((2, 2, z_n)),
                dma((2, 2, z_n)),
                dma((2 * z_n + 1,)),
                dma((2 * z_n + 1,)),
                dma((pairs, y_n)),
                dma((pairs, y_n)),
                dma((pairs,)),
                dma((pairs,)),
                dma((pairs,)),
                dma((pairs,)),
                dma((pairs, y_n)),
                dma((pairs, y_n)),
            ],
            compiler_params=pltpu.CompilerParams(
                collective_id=0, has_side_effects=True, vmem_limit_bytes=56 * 1024 * 1024
            ),
        )(
            text_len,
            step_size,
            jnp.transpose(attn_proj[0], (0, 2, 1, 3)),
            mlp_proj[0],
            stream[0],
            w_out_attn.T,
            w_out_mlp.T,
            w_final.T,
            jnp.asarray(cosine.reshape(rows, HEAD_DIM)),
            jnp.asarray(sine.reshape(rows, HEAD_DIM)),
            jnp.asarray(slot_number),
            q_gain[None],
            k_gain[None],
            bias_out[None],
            gate_mod,
            final_shift,
            final_scale,
            b_final[None],
            latent[0],
        )
        return hidden[None], latent_next[None]

    placed = (
        P("tile", None, "head", None, None),
        P("tile", None, "head", None),
        P("tile", None, "head", None),
        P("tile"),
        P(),
        P(),
        P("head", "tile"),
        P("head", "tile"),
        P(),
        P("tile", None),
        P("tile", None),
        P("tile", None),
        P(),
        P(),
        P("tile", None, "head", None),
        P("tile"),
    )
    return jax.shard_map(
        per_device,
        mesh=mesh,
        in_specs=placed,
        out_specs=(P("tile", None, "head", None), P("tile", None, "head", None)),
        check_vma=False,
    )
```

```python
import functools
import math

import jax
import jax.numpy as jnp
import numpy as np
from jax import lax
from jax.experimental import pallas as pl
from jax.experimental.pallas import tpu as pltpu
from jax.sharding import PartitionSpec as P

HEAD_DIM = 128
SLOTS = 192
GRID_W = 32
MESH = pl.DeviceIdType.MESH
F32 = jnp.float32
BF16 = jnp.bfloat16


def rope_constants(groups):
    zero = HEAD_DIM // 16
    axis = (HEAD_DIM // 2 - zero) // 2
    own = SLOTS // groups
    freqs = (10000.0 ** (-np.arange(axis, dtype=np.float32) / np.float32(axis))).astype(np.float32)
    angles = np.zeros((3, SLOTS, HEAD_DIM // 2), np.float32)
    for block in (1, 2):
        index = (block - 1) * SLOTS + np.arange(SLOTS)
        angles[block, :, zero : zero + axis] = (index // GRID_W).astype(np.float32)[:, None] * freqs
        angles[block, :, zero + axis :] = (index % GRID_W).astype(np.float32)[:, None] * freqs
    order = angles.reshape(3, groups, own, HEAD_DIM // 2).transpose(1, 0, 2, 3)
    wide = np.repeat(order.astype(np.float64), 2, axis=-1)
    sign = np.where(np.arange(HEAD_DIM) % 2 == 0, -1.0, 1.0)
    cosine = np.cos(wide).astype(np.float32)
    sine = (np.sin(wide) * sign).astype(np.float32)
    slot = np.full((3, SLOTS), -1, np.int32)
    slot[0] = np.arange(SLOTS)
    slot = slot.reshape(3, groups, own).transpose(1, 0, 2).reshape(1, -1)
    return cosine, sine, slot


def swap_pairs(x, even):
    return jnp.where(even, pltpu.roll(x, HEAD_DIM - 1, axis=x.ndim - 1), pltpu.roll(x, 1, axis=x.ndim - 1))


def layer_kernel(
    cfg,
    text_len,
    step_size,
    attn_in,
    mlp_in,
    stream_in,
    weight_attn,
    weight_mlp,
    w_final,
    cosine,
    sine,
    slot_number,
    q_gain,
    k_gain,
    bias_out,
    gate,
    shift,
    scale,
    b_final,
    latent,
    hidden_out,
    latent_out,
    got_attn,
    got_mlp,
    weights,
    queries,
    keys,
    values,
    mlp_act,
    act,
    product,
    y_out,
    y_in,
    y_low,
    y_sum,
    y_pass,
    y_got,
    x_out,
    x_in,
    x_pass,
    x_got,
    mine,
    updated,
    stream,
    final_w,
    table_c,
    table_s,
    local_sem,
    attn_send,
    attn_recv,
    mlp_send,
    mlp_recv,
    ring_send,
    ring_recv,
    side_send,
    side_recv,
    y_send,
    y_recv,
    y_low_send,
    y_low_recv,
    y_pass_send,
    y_pass_recv,
    x_send,
    x_recv,
    x_pass_send,
    x_pass_recv,
):
    heads_n, z_n, pairs, own_rows, own_slots = cfg
    y_n = heads_n // 2
    tile = lax.axis_index("tile")
    head = lax.axis_index("head")
    core = tile % 2
    depth = (tile // 2) % z_n
    half = tile // (2 * z_n)
    row_y = head // 2
    side_x = head % 2
    width = got_attn.shape[4]
    units = got_mlp.shape[3]
    local_heads = width // HEAD_DIM
    shard = weights.shape[1]
    columns = shard * 4
    rows = heads_n * own_rows

    def tile_at(half_, depth_, core_):
        return half_ * (2 * z_n) + depth_ * 2 + core_

    def shard_at(half_, depth_, core_):
        return depth_ * 4 + half_ * 2 + core_

    own_shard = shard_at(half, depth, core)
    up = tile_at(half, (depth + 1) % z_n, core)
    down = tile_at(half, (depth + z_n - 1) % z_n, core)
    across = tile_at(1 - half, depth, core)
    sibling = tile_at(half, depth, 1 - core)

    def head_at(dy, dx):
        return ((row_y + dy + y_n) % y_n) * 2 + (side_x + dx) % 2

    def peer_of(i):
        return head_at(i // 2, i % 2)

    def source_of(i):
        return head_at(-(i // 2), i % 2)

    def local_copies():
        at = pl.ds(pl.multiple_of(head * width, width), width)
        mt = pl.ds(pl.multiple_of(head * units, units), units)
        return [
            pltpu.make_async_copy(attn_in.at[:, :, :, at], got_attn.at[head], local_sem.at[0]),
            pltpu.make_async_copy(mlp_in.at[:, :, mt], got_mlp.at[head], local_sem.at[1]),
            pltpu.make_async_copy(weight_attn, weights.at[own_shard, :, pl.ds(0, width)], local_sem.at[2]),
            pltpu.make_async_copy(weight_mlp, weights.at[own_shard, :, pl.ds(width, units)], local_sem.at[3]),
            pltpu.make_async_copy(stream_in, stream, local_sem.at[4]),
            pltpu.make_async_copy(w_final, final_w, local_sem.at[5]),
        ]

    for copy in local_copies():
        copy.start()

    barrier = pltpu.get_barrier_semaphore()
    for neighbour in (up, down, across, sibling):
        pl.semaphore_signal(barrier, inc=1, device_id={"tile": neighbour}, device_id_type=MESH)

    def greet(i, _):
        pl.semaphore_signal(barrier, inc=1, device_id={"head": peer_of(i)}, device_id_type=MESH)
        return 0

    lax.fori_loop(1, heads_n, greet, 0)
    pl.semaphore_wait(barrier, heads_n - 1 + 4)

    def attn_copy(i, peer, source):
        return pltpu.make_async_remote_copy(
            src_ref=attn_in.at[:, :, :, pl.ds(pl.multiple_of(peer * width, width), width)],
            dst_ref=got_attn.at[source],
            send_sem=attn_send.at[i],
            recv_sem=attn_recv.at[i],
            device_id={"head": peer},
            device_id_type=MESH,
        )

    def mlp_copy(i, peer, source):
        return pltpu.make_async_remote_copy(
            src_ref=mlp_in.at[:, :, pl.ds(pl.multiple_of(peer * units, units), units)],
            dst_ref=got_mlp.at[source],
            send_sem=mlp_send.at[i],
            recv_sem=mlp_recv.at[i],
            device_id={"head": peer},
            device_id_type=MESH,
        )

    def send_attn(i, _):
        attn_copy(i, peer_of(i), head).start()
        return 0

    def send_mlp(i, _):
        mlp_copy(i, peer_of(i), head).start()
        return 0

    def ring_copy(stream_, direction, step, slot):
        return pltpu.make_async_remote_copy(
            src_ref=weights.at[slot],
            dst_ref=weights.at[slot],
            send_sem=ring_send.at[stream_, direction, step],
            recv_sem=ring_recv.at[stream_, direction, step],
            device_id={"tile": up if direction == 0 else down},
            device_id_type=MESH,
        )

    def side_copy(index, slot, to):
        return pltpu.make_async_remote_copy(
            src_ref=weights.at[slot],
            dst_ref=weights.at[slot],
            send_sem=side_send.at[index],
            recv_sem=side_recv.at[index],
            device_id={"tile": to},
            device_id_type=MESH,
        )

    far, near = z_n // 2, z_n - 1 - z_n // 2
    reach = ((far, near), (near, far))

    def half_of(stream_):
        return half if stream_ == 0 else 1 - half

    def arrival(stream_, direction, step):
        offset = z_n - step if direction == 0 else step
        slot = shard_at(half_of(stream_), (depth + offset) % z_n, core)
        return slot, stream_ * z_n + (offset if offset < z_n else 0)

    def begin(stream_):
        slot = shard_at(half_of(stream_), depth, core)
        ring_copy(stream_, 0, 1, slot).start()
        ring_copy(stream_, 1, 1, slot).start()
        side_copy(stream_ * z_n, slot, sibling).start()

    def advance(stream_, step):
        for direction in (0, 1):
            if step <= reach[stream_][direction]:
                slot, number = arrival(stream_, direction, step)
                ring_copy(stream_, direction, step, slot).wait_recv()
                if step < reach[stream_][direction]:
                    ring_copy(stream_, direction, step + 1, slot).start()
                side_copy(number, slot, sibling).start()

    cross = 2 * z_n
    locals_ = local_copies()
    locals_[2].wait()
    locals_[3].wait()
    side_copy(cross, own_shard, across).start()
    begin(0)
    lax.fori_loop(1, heads_n, send_attn, 0)
    lax.fori_loop(1, heads_n, send_mlp, 0)

    even = lax.broadcasted_iota(jnp.int32, (own_slots, HEAD_DIM), 1) % 2 == 0
    even8 = even[:8]
    for j, gain_ref in enumerate((q_gain, k_gain)):
        gain = jnp.broadcast_to(gain_ref[...], (8, HEAD_DIM))
        swapped = swap_pairs(gain, even8)[0:1]
        table_c[j] = cosine[...] * gain_ref[...]
        table_s[j] = sine[...] * swapped

    def prepare(group):
        for block in range(3):
            where = pl.ds(pl.multiple_of(group * own_rows + block * own_slots, 8), own_slots)
            for j, target in enumerate((queries, keys)):
                raw = got_attn[group, block, j].astype(F32)
                for n in range(local_heads):
                    x = raw[:, n * HEAD_DIM : (n + 1) * HEAD_DIM]
                    r = lax.rsqrt(jnp.mean(x * x, axis=-1, keepdims=True) + 1e-06)
                    y = r * (x * table_c[j, where] + swap_pairs(x, even) * table_s[j, where])
                    target[n, where] = y
            raw = got_attn[group, block, 2].astype(F32)
            for n in range(local_heads):
                values[n, where] = raw[:, n * HEAD_DIM : (n + 1) * HEAD_DIM]

    def receive_attn(i, _):
        source = source_of(i)
        attn_copy(i, head, source).wait_recv()
        prepare(source)
        return 0

    def activate(group):
        for block in range(3):
            where = pl.ds(pl.multiple_of(group * own_rows + block * own_slots, 8), own_slots)
            x = got_mlp[group, block].astype(F32)
            inner = math.sqrt(2.0 / math.pi) * (x + 0.044715 * (x * x * x))
            mlp_act[where] = 0.5 * x * (1.0 + jnp.tanh(inner))

    def receive_mlp(i, _):
        source = source_of(i)
        mlp_copy(i, head, source).wait_recv()
        activate(source)
        return 0

    live = slot_number[...] < text_len[0]
    factor = math.log2(math.e) / math.sqrt(HEAD_DIM)
    band = rows // 3

    def attend(n):
        k = keys[n].astype(BF16)
        v = values[n].astype(BF16)
        for part in range(3):
            q = queries[n, pl.ds(part * band, band)].astype(BF16)
            scores = lax.dot_general(q, k, (((1,), (1,)), ((), ())), preferred_element_type=F32)
            scores = jnp.where(live, scores, -1e30)
            top = jnp.max(scores, axis=-1, keepdims=True)
            weight = jnp.exp2((scores - top) * factor)
            total = jnp.sum(weight, axis=-1, keepdims=True)
            mixed = jnp.dot(weight.astype(BF16), v, preferred_element_type=F32)
            act[pl.ds(part * band, band), n * HEAD_DIM : (n + 1) * HEAD_DIM] = (mixed / total).astype(BF16)

    locals_[0].wait()
    prepare(head)
    side_copy(cross, shard_at(1 - half, depth, core), across).wait_recv()
    begin(1)
    advance(0, 1)
    advance(1, 1)
    lax.fori_loop(1, heads_n // 2, receive_attn, 0)
    lax.fori_loop(heads_n // 2, heads_n, receive_attn, 0)
    advance(0, 2)
    advance(1, 2)
    for n in range(local_heads):
        attend(n)
    locals_[1].wait()
    activate(head)
    lax.fori_loop(1, heads_n, receive_mlp, 0)
    act[:, width:] = mlp_act[...].astype(BF16)
    locals_[4].wait()
    locals_[5].wait()

    def wait_sibling(offsets):
        for stream_ in (0, 1):
            for offset in offsets:
                slot = shard_at(half_of(stream_), (depth + offset) % z_n, 1 - core)
                side_copy(stream_ * z_n + offset, slot, sibling).wait_recv()

    def first_of(p, y):
        odd = (p + core) % 2
        return (1 - odd) * (y + 1 - 2 * (y % 2)) + odd * (y_n - 1 - y)

    def y_copy(p):
        return pltpu.make_async_remote_copy(
            src_ref=y_out.at[p],
            dst_ref=y_in.at[p],
            send_sem=y_send.at[p],
            recv_sem=y_recv.at[p],
            device_id={"head": first_of(p, row_y) * 2 + side_x},
            device_id_type=MESH,
        )

    def y_low_copy(p):
        return pltpu.make_async_remote_copy(
            src_ref=y_low.at[p],
            dst_ref=y_sum.at[p],
            send_sem=y_low_send.at[p],
            recv_sem=y_low_recv.at[p],
            device_id={"head": first_of(p + 1, row_y) * 2 + side_x},
            device_id_type=MESH,
        )

    def y_pass_copy(p):
        return pltpu.make_async_remote_copy(
            src_ref=y_pass.at[p],
            dst_ref=y_got.at[p],
            send_sem=y_pass_send.at[p],
            recv_sem=y_pass_recv.at[p],
            device_id={"head": head_at(0, 1)},
            device_id_type=MESH,
        )

    def x_copy(p):
        return pltpu.make_async_remote_copy(
            src_ref=x_out.at[p],
            dst_ref=x_in.at[p],
            send_sem=x_send.at[p],
            recv_sem=x_recv.at[p],
            device_id={"head": head_at(0, 1)},
            device_id_type=MESH,
        )

    def x_pass_copy(p, dy):
        return pltpu.make_async_remote_copy(
            src_ref=x_pass.at[p, dy],
            dst_ref=x_got.at[p, dy],
            send_sem=x_pass_send.at[p, dy],
            recv_sem=x_pass_recv.at[p, dy],
            device_id={"head": head_at(dy, 0)},
            device_id_type=MESH,
        )

    def group_rows(kind, p, group):
        return product[kind, p, pl.ds(pl.multiple_of(group * own_rows, 8), own_rows)]

    def offset_of(kind, p):
        return p + 1 if kind == 1 else (z_n - p) % z_n

    def y_second(p):
        y_copy(p).wait_recv()
        other = first_of(p + 1, row_y)
        for side in (0, 1):
            total = group_rows(0, p, other * 2 + side) + y_in[p, 1, side].astype(F32)
            y_low[p, side] = total.astype(BF16)
        y_low_copy(p).start()

    def y_third(p):
        y_low_copy(p).wait_recv()
        for dx in (0, 1):
            side = (side_x + dx) % 2
            total = group_rows(0, p, row_y * 2 + side)
            total = total + y_in[p, 0, side].astype(F32) + y_sum[p, side].astype(F32)
            if dx == 0:
                mine[0, p] = total
            else:
                y_pass[p] = total.astype(BF16)
        y_pass_copy(p).start()

    def x_second(p):
        x_copy(p).wait_recv()
        for dy in range(1, y_n):
            peer_y = (row_y + dy) % y_n
            total = group_rows(1, p, peer_y * 2 + side_x) + x_in[p, peer_y].astype(F32)
            x_pass[p, dy] = total.astype(BF16)
            x_pass_copy(p, dy).start()
        mine[1, p] = group_rows(1, p, head) + x_in[p, row_y].astype(F32)

    wait_sibling([offset_of(kind, 0) for kind in (0, 1)])

    def project(k, _):
        p, kind = k // 2, 1 - k % 2

        @pl.when(k == 2)
        def _():
            wait_sibling([offset_of(kind, 1) for kind in (0, 1)])
            for step in range(3, far):
                advance(0, step)
                advance(1, step)

        @pl.when(k == 4)
        def _():
            wait_sibling([offset_of(kind, p) for p in range(2, pairs - 1) for kind in (0, 1)])

        @pl.when(k == 2 * pairs - 2)
        def _():
            y_second(0)
            advance(0, far)
            advance(1, far)
            wait_sibling([offset_of(kind, pairs - 1) for kind in (0, 1)])

        offset = kind * (p + 1) + (1 - kind) * ((z_n - p) % z_n)
        nearest = (depth + offset) % z_n
        block = weights[pl.ds(nearest * 4, 4)].reshape(columns, width + units)
        product[kind, p] = lax.dot_general(
            act[...], block, (((1,), (1,)), ((), ())), preferred_element_type=F32
        )

        @pl.when(kind == 0)
        def _():
            peer_y = first_of(p, row_y)
            for place, target in enumerate((peer_y, first_of(p + 1, peer_y))):
                for side in (0, 1):
                    y_out[p, place, side] = group_rows(0, p, target * 2 + side).astype(BF16)
            y_copy(p).start()

        @pl.when(kind == 1)
        def _():
            for peer_y in range(y_n):
                x_out[p, peer_y] = group_rows(1, p, peer_y * 2 + 1 - side_x).astype(BF16)
            x_copy(p).start()

        return 0

    lax.fori_loop(0, 2 * pairs, project, 0)

    def collect(p):
        y_pass_copy(p).wait_recv()
        mine[0, p] = mine[0, p] + y_got[p].astype(F32)
        total = mine[1, p]
        for dy in range(1, y_n):
            x_pass_copy(p, dy).wait_recv()
            total = total + x_got[p, dy].astype(F32)
        mine[1, p] = total

    x_second(0)
    y_second(1)
    y_third(0)
    y_second(2)
    x_second(1)
    y_third(1)
    y_second(3)
    x_second(2)
    y_third(2)
    y_third(3)
    x_second(3)
    collect(0)
    collect(1)
    collect(2)
    collect(3)

    def sum_at(z):
        offset = (z + z_n - depth) % z_n
        kind = (offset + z_n - 1) % z_n // pairs
        p = (1 - kind) * (offset - 1) + kind * ((z_n - offset) % z_n)
        return mine[1 - kind, p]

    narrow = columns // 2
    for pair in range(z_n // 2):
        low, high = sum_at(2 * pair), sum_at(2 * pair + 1)
        for side in (0, 1):
            piece = slice(side * narrow, (side + 1) * narrow)
            total = jnp.concatenate([low[:, piece], high[:, piece]], axis=-1)
            start = side * narrow * z_n + pair * columns
            at = slice(start, start + columns)
            for block in range(3):
                part = slice(block * own_slots, (block + 1) * own_slots)
                new = stream[block, :, at].astype(F32) + gate[:, at] * (total[part] + bias_out[:, at])
                updated[block, :, at] = new
                hidden_out[block, :, at] = new.astype(BF16)

    for block in (1, 2):
        image = updated[block]
        center = image - jnp.mean(image, axis=-1, keepdims=True)
        variance = jnp.mean(center * center, axis=-1, keepdims=True)
        normed = center * lax.rsqrt(variance + 1e-06)
        modulated = ((1.0 + scale[...]) * normed + shift[...]).astype(BF16)
        velocity = lax.dot_general(
            modulated, final_w[...], (((1,), (1,)), ((), ())), preferred_element_type=F32
        )
        latent_out[block - 1] = latent[block - 1] + step_size[0] * (velocity + b_final[...])

    def drain(i, _):
        attn_copy(i, peer_of(i), head).wait_send()
        mlp_copy(i, peer_of(i), head).wait_send()
        return 0

    lax.fori_loop(1, heads_n, drain, 0)

    def drain_parts(p, _):
        for dy in range(1, y_n):
            x_pass_copy(p, dy).wait_send()
        y_copy(p).wait_send()
        y_low_copy(p).wait_send()
        y_pass_copy(p).wait_send()
        x_copy(p).wait_send()
        return 0

    lax.fori_loop(0, pairs, drain_parts, 0)
    side_copy(cross, own_shard, across).wait_send()
    for stream_ in (0, 1):
        for offset in range(z_n):
            slot = shard_at(half_of(stream_), (depth + offset) % z_n, core)
            side_copy(stream_ * z_n + offset, slot, sibling).wait_send()
        for direction in (0, 1):
            for step in range(1, reach[stream_][direction] + 1):
                offset = z_n - step + 1 if direction == 0 else step - 1
                slot = shard_at(half_of(stream_), (depth + offset) % z_n, core)
                ring_copy(stream_, direction, step, slot).wait_send()


def solution(mesh):
    heads_n = mesh.shape["head"]
    tiles_n = mesh.shape["tile"]
    z_n = tiles_n // 4
    pairs = 4
    cosine, sine, slot_number = rope_constants(heads_n)

    def per_device(
        attn_proj,
        mlp_proj,
        stream,
        text_len,
        q_gain,
        k_gain,
        w_out_attn,
        w_out_mlp,
        bias_out,
        gate_mod,
        final_shift,
        final_scale,
        w_final,
        b_final,
        latent,
        step_size,
    ):
        own_slots = attn_proj.shape[2]
        own_rows = 3 * own_slots
        rows = heads_n * own_rows
        features = attn_proj.shape[4]
        width, shard = w_out_attn.shape
        units = w_out_mlp.shape[0]
        local_heads = width // HEAD_DIM
        columns = features // (2 * pairs)
        y_n = heads_n // 2
        channels = w_final.shape[1]
        cfg = (heads_n, z_n, pairs, own_rows, own_slots)
        any_ = pl.BlockSpec(memory_space=pl.ANY)
        vmem = pl.BlockSpec(memory_space=pltpu.VMEM)
        smem = pl.BlockSpec(memory_space=pltpu.SMEM)
        dma = pltpu.SemaphoreType.DMA
        hidden, latent_next = pl.pallas_call(
            functools.partial(layer_kernel, cfg),
            out_shape=(
                jax.ShapeDtypeStruct((3, own_slots, features), BF16),
                jax.ShapeDtypeStruct((2, own_slots, channels), F32),
            ),
            in_specs=[smem, smem] + [any_] * 6 + [vmem] * 11,
            out_specs=(vmem, vmem),
            scratch_shapes=[
                pltpu.VMEM((heads_n, 3, 3, own_slots, width), BF16),
                pltpu.VMEM((heads_n, 3, own_slots, units), BF16),
                pltpu.VMEM((tiles_n, shard, width + units), BF16),
                pltpu.VMEM((local_heads, rows, HEAD_DIM), F32),
                pltpu.VMEM((local_heads, rows, HEAD_DIM), F32),
                pltpu.VMEM((local_heads, rows, HEAD_DIM), F32),
                pltpu.VMEM((rows, units), F32),
                pltpu.VMEM((rows, width + units), BF16),
                pltpu.VMEM((2, pairs, rows, columns), F32),
                pltpu.VMEM((pairs, 2, 2, own_rows, columns), BF16),
                pltpu.VMEM((pairs, 2, 2, own_rows, columns), BF16),
                pltpu.VMEM((pairs, 2, own_rows, columns), BF16),
                pltpu.VMEM((pairs, 2, own_rows, columns), BF16),
                pltpu.VMEM((pairs, own_rows, columns), BF16),
                pltpu.VMEM((pairs, own_rows, columns), BF16),
                pltpu.VMEM((pairs, y_n, own_rows, columns), BF16),
                pltpu.VMEM((pairs, y_n, own_rows, columns), BF16),
                pltpu.VMEM((pairs, y_n, own_rows, columns), BF16),
                pltpu.VMEM((pairs, y_n, own_rows, columns), BF16),
                pltpu.VMEM((2, pairs, own_rows, columns), F32),
                pltpu.VMEM((3, own_slots, features), F32),
                pltpu.VMEM((3, own_slots, features), BF16),
                pltpu.VMEM((channels, features), BF16),
                pltpu.VMEM((2, rows, HEAD_DIM), F32),
                pltpu.VMEM((2, rows, HEAD_DIM), F32),
                dma((6,)),
                dma((heads_n,)),
                dma((heads_n,)),
                dma((heads_n,)),
                dma((heads_n,)),
                dma((2, 2, z_n)),
                dma((2, 2, z_n)),
                dma((2 * z_n + 1,)),
                dma((2 * z_n + 1,)),
                dma((pairs,)),
                dma((pairs,)),
                dma((pairs,)),
                dma((pairs,)),
                dma((pairs,)),
                dma((pairs,)),
                dma((pairs,)),
                dma((pairs,)),
                dma((pairs, y_n)),
                dma((pairs, y_n)),
            ],
            compiler_params=pltpu.CompilerParams(
                collective_id=0, has_side_effects=True, vmem_limit_bytes=56 * 1024 * 1024
            ),
        )(
            text_len,
            step_size,
            jnp.transpose(attn_proj[0], (0, 2, 1, 3)),
            mlp_proj[0],
            stream[0],
            w_out_attn.T,
            w_out_mlp.T,
            w_final.T,
            jnp.asarray(cosine.reshape(rows, HEAD_DIM)),
            jnp.asarray(sine.reshape(rows, HEAD_DIM)),
            jnp.asarray(slot_number),
            q_gain[None],
            k_gain[None],
            bias_out[None],
            gate_mod,
            final_shift,
            final_scale,
            b_final[None],
            latent[0],
        )
        return hidden[None], latent_next[None]

    placed = (
        P("tile", None, "head", None, None),
        P("tile", None, "head", None),
        P("tile", None, "head", None),
        P("tile"),
        P(),
        P(),
        P("head", "tile"),
        P("head", "tile"),
        P(),
        P("tile", None),
        P("tile", None),
        P("tile", None),
        P(),
        P(),
        P("tile", None, "head", None),
        P("tile"),
    )
    return jax.shard_map(
        per_device,
        mesh=mesh,
        in_specs=placed,
        out_specs=(P("tile", None, "head", None), P("tile", None, "head", None)),
        check_vma=False,
    )
```

```python
import functools
import math

import jax
import jax.numpy as jnp
import numpy as np
from jax import lax
from jax.experimental import pallas as pl
from jax.experimental.pallas import tpu as pltpu
from jax.sharding import PartitionSpec as P

HEAD_DIM = 128
SLOTS = 192
GRID_W = 32
MESH = pl.DeviceIdType.MESH
F32 = jnp.float32
BF16 = jnp.bfloat16


def rope_constants(groups):
    zero = HEAD_DIM // 16
    axis = (HEAD_DIM // 2 - zero) // 2
    own = SLOTS // groups
    freqs = (10000.0 ** (-np.arange(axis, dtype=np.float32) / np.float32(axis))).astype(np.float32)
    angles = np.zeros((3, SLOTS, HEAD_DIM // 2), np.float32)
    for block in (1, 2):
        index = (block - 1) * SLOTS + np.arange(SLOTS)
        angles[block, :, zero : zero + axis] = (index // GRID_W).astype(np.float32)[:, None] * freqs
        angles[block, :, zero + axis :] = (index % GRID_W).astype(np.float32)[:, None] * freqs
    order = angles.reshape(3, groups, own, HEAD_DIM // 2).transpose(1, 0, 2, 3)
    wide = np.repeat(order.astype(np.float64), 2, axis=-1)
    sign = np.where(np.arange(HEAD_DIM) % 2 == 0, -1.0, 1.0)
    cosine = np.cos(wide).astype(np.float32)
    sine = (np.sin(wide) * sign).astype(np.float32)
    slot = np.full((3, SLOTS), -1, np.int32)
    slot[0] = np.arange(SLOTS)
    slot = slot.reshape(3, groups, own).transpose(1, 0, 2).reshape(1, -1)
    return cosine, sine, slot


def swap_pairs(x, even):
    return jnp.where(even, pltpu.roll(x, HEAD_DIM - 1, axis=x.ndim - 1), pltpu.roll(x, 1, axis=x.ndim - 1))


def layer_kernel(
    cfg,
    text_len,
    step_size,
    attn_in,
    mlp_in,
    stream_in,
    weight_attn,
    weight_mlp,
    w_final,
    cosine,
    sine,
    slot_number,
    q_gain,
    k_gain,
    bias_out,
    gate,
    shift,
    scale,
    b_final,
    latent,
    hidden_out,
    latent_out,
    got_attn,
    got_mlp,
    weights,
    queries,
    keys,
    values,
    mlp_act,
    act,
    product,
    y_out,
    y_in,
    y_low,
    y_sum,
    y_pass,
    y_got,
    x_out,
    x_in,
    x_pass,
    x_got,
    mine,
    updated,
    stream,
    final_w,
    table_c,
    table_s,
    local_sem,
    attn_send,
    attn_recv,
    mlp_send,
    mlp_recv,
    ring_send,
    ring_recv,
    side_send,
    side_recv,
    y_send,
    y_recv,
    y_low_send,
    y_low_recv,
    y_pass_send,
    y_pass_recv,
    x_send,
    x_recv,
    x_pass_send,
    x_pass_recv,
):
    heads_n, z_n, pairs, own_rows, own_slots = cfg
    y_n = heads_n // 2
    tile = lax.axis_index("tile")
    head = lax.axis_index("head")
    core = tile % 2
    depth = (tile // 2) % z_n
    half = tile // (2 * z_n)
    row_y = head // 2
    side_x = head % 2
    width = got_attn.shape[4]
    units = got_mlp.shape[3]
    local_heads = width // HEAD_DIM
    shard = weights.shape[1]
    columns = shard * 4
    rows = heads_n * own_rows

    def tile_at(half_, depth_, core_):
        return half_ * (2 * z_n) + depth_ * 2 + core_

    def shard_at(half_, depth_, core_):
        return depth_ * 4 + half_ * 2 + core_

    own_shard = shard_at(half, depth, core)
    up = tile_at(half, (depth + 1) % z_n, core)
    down = tile_at(half, (depth + z_n - 1) % z_n, core)
    across = tile_at(1 - half, depth, core)
    sibling = tile_at(half, depth, 1 - core)

    def head_at(dy, dx):
        return ((row_y + dy + y_n) % y_n) * 2 + (side_x + dx) % 2

    def peer_of(i):
        return head_at(i // 2, i % 2)

    def source_of(i):
        return head_at(-(i // 2), i % 2)

    def local_copies():
        at = pl.ds(pl.multiple_of(head * width, width), width)
        mt = pl.ds(pl.multiple_of(head * units, units), units)
        return [
            pltpu.make_async_copy(attn_in.at[:, :, :, at], got_attn.at[head], local_sem.at[0]),
            pltpu.make_async_copy(mlp_in.at[:, :, mt], got_mlp.at[head], local_sem.at[1]),
            pltpu.make_async_copy(weight_attn, weights.at[own_shard, :, pl.ds(0, width)], local_sem.at[2]),
            pltpu.make_async_copy(weight_mlp, weights.at[own_shard, :, pl.ds(width, units)], local_sem.at[3]),
            pltpu.make_async_copy(stream_in, stream, local_sem.at[4]),
            pltpu.make_async_copy(w_final, final_w, local_sem.at[5]),
        ]

    for copy in local_copies():
        copy.start()

    barrier = pltpu.get_barrier_semaphore()
    for neighbour in (up, down, across, sibling):
        pl.semaphore_signal(barrier, inc=1, device_id={"tile": neighbour}, device_id_type=MESH)

    def greet(i, _):
        pl.semaphore_signal(barrier, inc=1, device_id={"head": peer_of(i)}, device_id_type=MESH)
        return 0

    lax.fori_loop(1, heads_n, greet, 0)
    pl.semaphore_wait(barrier, heads_n - 1 + 4)

    def attn_copy(i, peer, source):
        return pltpu.make_async_remote_copy(
            src_ref=attn_in.at[:, :, :, pl.ds(pl.multiple_of(peer * width, width), width)],
            dst_ref=got_attn.at[source],
            send_sem=attn_send.at[i],
            recv_sem=attn_recv.at[i],
            device_id={"head": peer},
            device_id_type=MESH,
        )

    def mlp_copy(i, peer, source):
        return pltpu.make_async_remote_copy(
            src_ref=mlp_in.at[:, :, pl.ds(pl.multiple_of(peer * units, units), units)],
            dst_ref=got_mlp.at[source],
            send_sem=mlp_send.at[i],
            recv_sem=mlp_recv.at[i],
            device_id={"head": peer},
            device_id_type=MESH,
        )

    def send_attn(i, _):
        attn_copy(i, peer_of(i), head).start()
        return 0

    def send_mlp(i, _):
        mlp_copy(i, peer_of(i), head).start()
        return 0

    def ring_copy(stream_, direction, step, slot):
        return pltpu.make_async_remote_copy(
            src_ref=weights.at[slot],
            dst_ref=weights.at[slot],
            send_sem=ring_send.at[stream_, direction, step],
            recv_sem=ring_recv.at[stream_, direction, step],
            device_id={"tile": up if direction == 0 else down},
            device_id_type=MESH,
        )

    def side_copy(index, slot, to):
        return pltpu.make_async_remote_copy(
            src_ref=weights.at[slot],
            dst_ref=weights.at[slot],
            send_sem=side_send.at[index],
            recv_sem=side_recv.at[index],
            device_id={"tile": to},
            device_id_type=MESH,
        )

    far, near = z_n // 2, z_n - 1 - z_n // 2
    reach = ((far, near), (near, far))

    def half_of(stream_):
        return half if stream_ == 0 else 1 - half

    def arrival(stream_, direction, step):
        offset = z_n - step if direction == 0 else step
        slot = shard_at(half_of(stream_), (depth + offset) % z_n, core)
        return slot, stream_ * z_n + (offset if offset < z_n else 0)

    def begin(stream_):
        slot = shard_at(half_of(stream_), depth, core)
        ring_copy(stream_, 0, 1, slot).start()
        ring_copy(stream_, 1, 1, slot).start()
        side_copy(stream_ * z_n, slot, sibling).start()

    def advance(stream_, step):
        for direction in (0, 1):
            if step <= reach[stream_][direction]:
                slot, number = arrival(stream_, direction, step)
                ring_copy(stream_, direction, step, slot).wait_recv()
                if step < reach[stream_][direction]:
                    ring_copy(stream_, direction, step + 1, slot).start()
                side_copy(number, slot, sibling).start()

    cross = 2 * z_n
    locals_ = local_copies()
    locals_[2].wait()
    locals_[3].wait()
    side_copy(cross, own_shard, across).start()
    begin(0)
    lax.fori_loop(1, heads_n, send_attn, 0)
    lax.fori_loop(1, heads_n, send_mlp, 0)

    even = lax.broadcasted_iota(jnp.int32, (own_slots, HEAD_DIM), 1) % 2 == 0
    even8 = even[:8]
    for j, gain_ref in enumerate((q_gain, k_gain)):
        gain = jnp.broadcast_to(gain_ref[...], (8, HEAD_DIM))
        swapped = swap_pairs(gain, even8)[0:1]
        table_c[j] = cosine[...] * gain_ref[...]
        table_s[j] = sine[...] * swapped

    def prepare(group):
        for block in range(3):
            where = pl.ds(pl.multiple_of(group * own_rows + block * own_slots, 8), own_slots)
            for j, target in enumerate((queries, keys)):
                raw = got_attn[group, block, j].astype(F32)
                for n in range(local_heads):
                    x = raw[:, n * HEAD_DIM : (n + 1) * HEAD_DIM]
                    r = lax.rsqrt(jnp.mean(x * x, axis=-1, keepdims=True) + 1e-06)
                    y = r * (x * table_c[j, where] + swap_pairs(x, even) * table_s[j, where])
                    target[n, where] = y
            raw = got_attn[group, block, 2].astype(F32)
            for n in range(local_heads):
                values[n, where] = raw[:, n * HEAD_DIM : (n + 1) * HEAD_DIM]

    def receive_attn(i, _):
        source = source_of(i)
        attn_copy(i, head, source).wait_recv()
        prepare(source)
        return 0

    def activate(group):
        for block in range(3):
            where = pl.ds(pl.multiple_of(group * own_rows + block * own_slots, 8), own_slots)
            x = got_mlp[group, block].astype(F32)
            inner = math.sqrt(2.0 / math.pi) * (x + 0.044715 * (x * x * x))
            mlp_act[where] = 0.5 * x * (1.0 + jnp.tanh(inner))

    def receive_mlp(i, _):
        source = source_of(i)
        mlp_copy(i, head, source).wait_recv()
        activate(source)
        return 0

    live = slot_number[...] < text_len[0]
    factor = math.log2(math.e) / math.sqrt(HEAD_DIM)
    band = rows // 3

    def attend(n):
        k = keys[n].astype(BF16)
        v = values[n].astype(BF16)
        for part in range(3):
            q = queries[n, pl.ds(part * band, band)].astype(BF16)
            scores = lax.dot_general(q, k, (((1,), (1,)), ((), ())), preferred_element_type=F32)
            scores = jnp.where(live, scores, -1e30)
            top = jnp.max(scores, axis=-1, keepdims=True)
            weight = jnp.exp2((scores - top) * factor)
            total = jnp.sum(weight, axis=-1, keepdims=True)
            mixed = jnp.dot(weight.astype(BF16), v, preferred_element_type=F32)
            act[pl.ds(part * band, band), n * HEAD_DIM : (n + 1) * HEAD_DIM] = (mixed / total).astype(BF16)

    locals_[0].wait()
    prepare(head)
    side_copy(cross, shard_at(1 - half, depth, core), across).wait_recv()
    begin(1)
    advance(0, 1)
    advance(1, 1)
    lax.fori_loop(1, heads_n // 2, receive_attn, 0)
    lax.fori_loop(heads_n // 2, heads_n, receive_attn, 0)
    advance(0, 2)
    advance(1, 2)
    for n in range(local_heads):
        attend(n)
    locals_[1].wait()
    activate(head)
    lax.fori_loop(1, heads_n, receive_mlp, 0)
    act[:, width:] = mlp_act[...].astype(BF16)
    locals_[4].wait()
    locals_[5].wait()

    def wait_sibling(offsets):
        for stream_ in (0, 1):
            for offset in offsets:
                slot = shard_at(half_of(stream_), (depth + offset) % z_n, 1 - core)
                side_copy(stream_ * z_n + offset, slot, sibling).wait_recv()

    def first_of(p, y):
        odd = (p + core) % 2
        return (1 - odd) * (y + 1 - 2 * (y % 2)) + odd * (y_n - 1 - y)

    def y_copy(p):
        return pltpu.make_async_remote_copy(
            src_ref=y_out.at[p],
            dst_ref=y_in.at[p],
            send_sem=y_send.at[p],
            recv_sem=y_recv.at[p],
            device_id={"head": first_of(p, row_y) * 2 + side_x},
            device_id_type=MESH,
        )

    def y_low_copy(p):
        return pltpu.make_async_remote_copy(
            src_ref=y_low.at[p],
            dst_ref=y_sum.at[p],
            send_sem=y_low_send.at[p],
            recv_sem=y_low_recv.at[p],
            device_id={"head": first_of(p + 1, row_y) * 2 + side_x},
            device_id_type=MESH,
        )

    def y_pass_copy(p):
        return pltpu.make_async_remote_copy(
            src_ref=y_pass.at[p],
            dst_ref=y_got.at[p],
            send_sem=y_pass_send.at[p],
            recv_sem=y_pass_recv.at[p],
            device_id={"head": head_at(0, 1)},
            device_id_type=MESH,
        )

    def x_copy(p):
        return pltpu.make_async_remote_copy(
            src_ref=x_out.at[p],
            dst_ref=x_in.at[p],
            send_sem=x_send.at[p],
            recv_sem=x_recv.at[p],
            device_id={"head": head_at(0, 1)},
            device_id_type=MESH,
        )

    def x_pass_copy(p, dy):
        return pltpu.make_async_remote_copy(
            src_ref=x_pass.at[p, dy],
            dst_ref=x_got.at[p, dy],
            send_sem=x_pass_send.at[p, dy],
            recv_sem=x_pass_recv.at[p, dy],
            device_id={"head": head_at(dy, 0)},
            device_id_type=MESH,
        )

    def group_rows(kind, p, group):
        return product[kind, p, pl.ds(pl.multiple_of(group * own_rows, 8), own_rows)]

    def offset_of(kind, p):
        return p + 1 if kind == 1 else (z_n - p) % z_n

    def y_second(p):
        y_copy(p).wait_recv()
        other = first_of(p + 1, row_y)
        for side in (0, 1):
            total = group_rows(0, p, other * 2 + side) + y_in[p, 1, side].astype(F32)
            y_low[p, side] = total.astype(BF16)
        y_low_copy(p).start()

    def y_third(p):
        y_low_copy(p).wait_recv()
        for dx in (0, 1):
            side = (side_x + dx) % 2
            total = group_rows(0, p, row_y * 2 + side)
            total = total + y_in[p, 0, side].astype(F32) + y_sum[p, side].astype(F32)
            if dx == 0:
                mine[0, p] = total
            else:
                y_pass[p] = total.astype(BF16)
        y_pass_copy(p).start()

    def x_second(p):
        x_copy(p).wait_recv()
        for dy in range(1, y_n):
            peer_y = (row_y + dy) % y_n
            total = group_rows(1, p, peer_y * 2 + side_x) + x_in[p, peer_y].astype(F32)
            x_pass[p, dy] = total.astype(BF16)
            x_pass_copy(p, dy).start()
        mine[1, p] = group_rows(1, p, head) + x_in[p, row_y].astype(F32)

    wait_sibling([offset_of(kind, 0) for kind in (0, 1)])

    def project(k, _):
        p, kind = k // 2, 1 - k % 2

        @pl.when(k == 2)
        def _():
            wait_sibling([offset_of(kind, 1) for kind in (0, 1)])
            for step in range(3, far):
                advance(0, step)
                advance(1, step)

        @pl.when(k == 4)
        def _():
            wait_sibling([offset_of(kind, p) for p in range(2, pairs - 1) for kind in (0, 1)])

        @pl.when(k == 2 * pairs - 2)
        def _():
            y_second(0)
            advance(0, far)
            advance(1, far)
            wait_sibling([offset_of(kind, pairs - 1) for kind in (0, 1)])

        offset = kind * (p + 1) + (1 - kind) * ((z_n - p) % z_n)
        nearest = (depth + offset) % z_n
        block = weights[pl.ds(nearest * 4, 4)].reshape(columns, width + units)
        product[kind, p] = lax.dot_general(
            act[...], block, (((1,), (1,)), ((), ())), preferred_element_type=F32
        )

        @pl.when(kind == 0)
        def _():
            peer_y = first_of(p, row_y)
            for place, target in enumerate((peer_y, first_of(p + 1, peer_y))):
                for side in (0, 1):
                    y_out[p, place, side] = group_rows(0, p, target * 2 + side).astype(BF16)
            y_copy(p).start()

        @pl.when(kind == 1)
        def _():
            for peer_y in range(y_n):
                x_out[p, peer_y] = group_rows(1, p, peer_y * 2 + 1 - side_x).astype(BF16)
            x_copy(p).start()

        return 0

    lax.fori_loop(0, 2 * pairs, project, 0)

    def collect(p):
        y_pass_copy(p).wait_recv()
        mine[0, p] = mine[0, p] + y_got[p].astype(F32)
        total = mine[1, p]
        for dy in range(1, y_n):
            x_pass_copy(p, dy).wait_recv()
            total = total + x_got[p, dy].astype(F32)
        mine[1, p] = total

    x_second(0)
    y_second(1)
    y_third(0)
    y_second(2)
    x_second(1)
    y_third(1)
    y_second(3)
    x_second(2)
    y_third(2)
    y_third(3)
    x_second(3)
    collect(0)
    collect(1)
    collect(2)
    collect(3)

    def sum_at(z):
        offset = (z + z_n - depth) % z_n
        kind = (offset + z_n - 1) % z_n // pairs
        p = (1 - kind) * (offset - 1) + kind * ((z_n - offset) % z_n)
        return mine[1 - kind, p]

    narrow = columns // 2
    for pair in range(z_n // 2):
        low, high = sum_at(2 * pair), sum_at(2 * pair + 1)
        for side in (0, 1):
            piece = slice(side * narrow, (side + 1) * narrow)
            total = jnp.concatenate([low[:, piece], high[:, piece]], axis=-1)
            start = side * narrow * z_n + pair * columns
            at = slice(start, start + columns)
            for block in range(3):
                part = slice(block * own_slots, (block + 1) * own_slots)
                new = stream[block, :, at].astype(F32) + gate[:, at] * (total[part] + bias_out[:, at])
                updated[block, :, at] = new
                hidden_out[block, :, at] = new.astype(BF16)

    for block in (1, 2):
        image = updated[block]
        center = image - jnp.mean(image, axis=-1, keepdims=True)
        variance = jnp.mean(center * center, axis=-1, keepdims=True)
        normed = center * lax.rsqrt(variance + 1e-06)
        modulated = ((1.0 + scale[...]) * normed + shift[...]).astype(BF16)
        velocity = lax.dot_general(
            modulated, final_w[...], (((1,), (1,)), ((), ())), preferred_element_type=F32
        )
        latent_out[block - 1] = latent[block - 1] + step_size[0] * (velocity + b_final[...])

    def drain(i, _):
        attn_copy(i, peer_of(i), head).wait_send()
        mlp_copy(i, peer_of(i), head).wait_send()
        return 0

    lax.fori_loop(1, heads_n, drain, 0)

    def drain_parts(p, _):
        for dy in range(1, y_n):
            x_pass_copy(p, dy).wait_send()
        y_copy(p).wait_send()
        y_low_copy(p).wait_send()
        y_pass_copy(p).wait_send()
        x_copy(p).wait_send()
        return 0

    lax.fori_loop(0, pairs, drain_parts, 0)
    side_copy(cross, own_shard, across).wait_send()
    for stream_ in (0, 1):
        for offset in range(z_n):
            slot = shard_at(half_of(stream_), (depth + offset) % z_n, core)
            side_copy(stream_ * z_n + offset, slot, sibling).wait_send()
        for direction in (0, 1):
            for step in range(1, reach[stream_][direction] + 1):
                offset = z_n - step + 1 if direction == 0 else step - 1
                slot = shard_at(half_of(stream_), (depth + offset) % z_n, core)
                ring_copy(stream_, direction, step, slot).wait_send()


def hand_on(hidden_in, latent_in, hidden_out, latent_out):
    hidden_out[...] = hidden_in[...]
    latent_out[...] = latent_in[...]


def solution(mesh):
    heads_n = mesh.shape["head"]
    tiles_n = mesh.shape["tile"]
    z_n = tiles_n // 4
    pairs = 4
    cosine, sine, slot_number = rope_constants(heads_n)

    def per_device(
        attn_proj,
        mlp_proj,
        stream,
        text_len,
        q_gain,
        k_gain,
        w_out_attn,
        w_out_mlp,
        bias_out,
        gate_mod,
        final_shift,
        final_scale,
        w_final,
        b_final,
        latent,
        step_size,
    ):
        own_slots = attn_proj.shape[2]
        own_rows = 3 * own_slots
        rows = heads_n * own_rows
        features = attn_proj.shape[4]
        width, shard = w_out_attn.shape
        units = w_out_mlp.shape[0]
        local_heads = width // HEAD_DIM
        columns = features // (2 * pairs)
        y_n = heads_n // 2
        channels = w_final.shape[1]
        cfg = (heads_n, z_n, pairs, own_rows, own_slots)
        any_ = pl.BlockSpec(memory_space=pl.ANY)
        vmem = pl.BlockSpec(memory_space=pltpu.VMEM)
        smem = pl.BlockSpec(memory_space=pltpu.SMEM)
        dma = pltpu.SemaphoreType.DMA
        hidden, latent_next = pl.pallas_call(
            functools.partial(layer_kernel, cfg),
            out_shape=(
                jax.ShapeDtypeStruct((3, own_slots, features), BF16),
                jax.ShapeDtypeStruct((2, own_slots, channels), F32),
            ),
            in_specs=[smem, smem] + [any_] * 6 + [vmem] * 11,
            out_specs=(vmem, vmem),
            scratch_shapes=[
                pltpu.VMEM((heads_n, 3, 3, own_slots, width), BF16),
                pltpu.VMEM((heads_n, 3, own_slots, units), BF16),
                pltpu.VMEM((tiles_n, shard, width + units), BF16),
                pltpu.VMEM((local_heads, rows, HEAD_DIM), F32),
                pltpu.VMEM((local_heads, rows, HEAD_DIM), F32),
                pltpu.VMEM((local_heads, rows, HEAD_DIM), F32),
                pltpu.VMEM((rows, units), F32),
                pltpu.VMEM((rows, width + units), BF16),
                pltpu.VMEM((2, pairs, rows, columns), F32),
                pltpu.VMEM((pairs, 2, 2, own_rows, columns), BF16),
                pltpu.VMEM((pairs, 2, 2, own_rows, columns), BF16),
                pltpu.VMEM((pairs, 2, own_rows, columns), BF16),
                pltpu.VMEM((pairs, 2, own_rows, columns), BF16),
                pltpu.VMEM((pairs, own_rows, columns), BF16),
                pltpu.VMEM((pairs, own_rows, columns), BF16),
                pltpu.VMEM((pairs, y_n, own_rows, columns), BF16),
                pltpu.VMEM((pairs, y_n, own_rows, columns), BF16),
                pltpu.VMEM((pairs, y_n, own_rows, columns), BF16),
                pltpu.VMEM((pairs, y_n, own_rows, columns), BF16),
                pltpu.VMEM((2, pairs, own_rows, columns), F32),
                pltpu.VMEM((3, own_slots, features), F32),
                pltpu.VMEM((3, own_slots, features), BF16),
                pltpu.VMEM((channels, features), BF16),
                pltpu.VMEM((2, rows, HEAD_DIM), F32),
                pltpu.VMEM((2, rows, HEAD_DIM), F32),
                dma((6,)),
                dma((heads_n,)),
                dma((heads_n,)),
                dma((heads_n,)),
                dma((heads_n,)),
                dma((2, 2, z_n)),
                dma((2, 2, z_n)),
                dma((2 * z_n + 1,)),
                dma((2 * z_n + 1,)),
                dma((pairs,)),
                dma((pairs,)),
                dma((pairs,)),
                dma((pairs,)),
                dma((pairs,)),
                dma((pairs,)),
                dma((pairs,)),
                dma((pairs,)),
                dma((pairs, y_n)),
                dma((pairs, y_n)),
            ],
            compiler_params=pltpu.CompilerParams(
                collective_id=0, has_side_effects=True, vmem_limit_bytes=56 * 1024 * 1024
            ),
        )(
            text_len,
            step_size,
            jnp.transpose(attn_proj[0], (0, 2, 1, 3)),
            mlp_proj[0],
            stream[0],
            w_out_attn.T,
            w_out_mlp.T,
            w_final.T,
            jnp.asarray(cosine.reshape(rows, HEAD_DIM)),
            jnp.asarray(sine.reshape(rows, HEAD_DIM)),
            jnp.asarray(slot_number),
            q_gain[None],
            k_gain[None],
            bias_out[None],
            gate_mod,
            final_shift,
            final_scale,
            b_final[None],
            latent[0],
        )
        hidden, latent_next = pl.pallas_call(
            hand_on,
            out_shape=(
                jax.ShapeDtypeStruct(hidden.shape, hidden.dtype),
                jax.ShapeDtypeStruct(latent_next.shape, latent_next.dtype),
            ),
            in_specs=[vmem, vmem],
            out_specs=(vmem, vmem),
        )(hidden, latent_next)
        return hidden[None], latent_next[None]

    placed = (
        P("tile", None, "head", None, None),
        P("tile", None, "head", None),
        P("tile", None, "head", None),
        P("tile"),
        P(),
        P(),
        P("head", "tile"),
        P("head", "tile"),
        P(),
        P("tile", None),
        P("tile", None),
        P("tile", None),
        P(),
        P(),
        P("tile", None, "head", None),
        P("tile"),
    )
    return jax.shard_map(
        per_device,
        mesh=mesh,
        in_specs=placed,
        out_specs=(P("tile", None, "head", None), P("tile", None, "head", None)),
        check_vma=False,
    )
```

```python
import functools
import math

import jax
import jax.numpy as jnp
import numpy as np
from jax import lax
from jax.experimental import pallas as pl
from jax.experimental.pallas import tpu as pltpu
from jax.sharding import PartitionSpec as P

HEAD_DIM = 128
SLOTS = 192
GRID_W = 32
MESH = pl.DeviceIdType.MESH
F32 = jnp.float32
BF16 = jnp.bfloat16


def rope_constants(groups):
    zero = HEAD_DIM // 16
    axis = (HEAD_DIM // 2 - zero) // 2
    own = SLOTS // groups
    freqs = (10000.0 ** (-np.arange(axis, dtype=np.float32) / np.float32(axis))).astype(np.float32)
    angles = np.zeros((3, SLOTS, HEAD_DIM // 2), np.float32)
    for block in (1, 2):
        index = (block - 1) * SLOTS + np.arange(SLOTS)
        angles[block, :, zero : zero + axis] = (index // GRID_W).astype(np.float32)[:, None] * freqs
        angles[block, :, zero + axis :] = (index % GRID_W).astype(np.float32)[:, None] * freqs
    order = angles.reshape(3, groups, own, HEAD_DIM // 2).transpose(1, 0, 2, 3)
    wide = np.repeat(order.astype(np.float64), 2, axis=-1)
    sign = np.where(np.arange(HEAD_DIM) % 2 == 0, -1.0, 1.0)
    cosine = np.cos(wide).astype(np.float32)
    sine = (np.sin(wide) * sign).astype(np.float32)
    slot = np.full((3, SLOTS), -1, np.int32)
    slot[0] = np.arange(SLOTS)
    slot = slot.reshape(3, groups, own).transpose(1, 0, 2).reshape(1, -1)
    return cosine, sine, slot


def swap_pairs(x, even):
    return jnp.where(even, pltpu.roll(x, HEAD_DIM - 1, axis=x.ndim - 1), pltpu.roll(x, 1, axis=x.ndim - 1))


def layer_kernel(
    cfg,
    text_len,
    step_size,
    attn_in,
    mlp_in,
    stream_in,
    weight_attn,
    weight_mlp,
    w_final,
    cosine,
    sine,
    slot_number,
    q_gain,
    k_gain,
    bias_out,
    gate,
    shift,
    scale,
    b_final,
    latent,
    hidden_out,
    latent_out,
    got_attn,
    got_mlp,
    weights,
    queries,
    keys,
    values,
    mlp_act,
    act,
    product,
    y_out,
    y_in,
    y_low,
    y_sum,
    y_pass,
    y_got,
    x_out,
    x_in,
    x_pass,
    x_got,
    mine,
    updated,
    stream,
    final_w,
    table_c,
    table_s,
    local_sem,
    attn_send,
    attn_recv,
    mlp_send,
    mlp_recv,
    ring_send,
    ring_recv,
    side_send,
    side_recv,
    y_send,
    y_recv,
    y_low_send,
    y_low_recv,
    y_pass_send,
    y_pass_recv,
    x_send,
    x_recv,
    x_pass_send,
    x_pass_recv,
):
    heads_n, z_n, pairs, own_rows, own_slots = cfg
    y_n = heads_n // 2
    tile = lax.axis_index("tile")
    head = lax.axis_index("head")
    core = tile % 2
    depth = (tile // 2) % z_n
    half = tile // (2 * z_n)
    row_y = head // 2
    side_x = head % 2
    width = got_attn.shape[4]
    units = got_mlp.shape[3]
    local_heads = width // HEAD_DIM
    shard = weights.shape[1]
    columns = shard * 4
    rows = heads_n * own_rows

    def tile_at(half_, depth_, core_):
        return half_ * (2 * z_n) + depth_ * 2 + core_

    def shard_at(half_, depth_, core_):
        return depth_ * 4 + half_ * 2 + core_

    own_shard = shard_at(half, depth, core)
    up = tile_at(half, (depth + 1) % z_n, core)
    down = tile_at(half, (depth + z_n - 1) % z_n, core)
    across = tile_at(1 - half, depth, core)
    sibling = tile_at(half, depth, 1 - core)

    def head_at(dy, dx):
        return ((row_y + dy + y_n) % y_n) * 2 + (side_x + dx) % 2

    def peer_of(i):
        return head_at(i // 2, i % 2)

    def source_of(i):
        return head_at(-(i // 2), i % 2)

    def local_copies():
        at = pl.ds(pl.multiple_of(head * width, width), width)
        mt = pl.ds(pl.multiple_of(head * units, units), units)
        return [
            pltpu.make_async_copy(attn_in.at[:, :, :, at], got_attn.at[head], local_sem.at[0]),
            pltpu.make_async_copy(mlp_in.at[:, :, mt], got_mlp.at[head], local_sem.at[1]),
            pltpu.make_async_copy(weight_attn, weights.at[own_shard, :, pl.ds(0, width)], local_sem.at[2]),
            pltpu.make_async_copy(weight_mlp, weights.at[own_shard, :, pl.ds(width, units)], local_sem.at[3]),
            pltpu.make_async_copy(stream_in, stream, local_sem.at[4]),
            pltpu.make_async_copy(w_final, final_w, local_sem.at[5]),
        ]

    for copy in local_copies():
        copy.start()

    barrier = pltpu.get_barrier_semaphore()
    for neighbour in (up, down, across, sibling):
        pl.semaphore_signal(barrier, inc=1, device_id={"tile": neighbour}, device_id_type=MESH)

    def greet(i, _):
        pl.semaphore_signal(barrier, inc=1, device_id={"head": peer_of(i)}, device_id_type=MESH)
        return 0

    lax.fori_loop(1, heads_n, greet, 0)
    pl.semaphore_wait(barrier, heads_n - 1 + 4)

    def attn_copy(i, peer, source):
        return pltpu.make_async_remote_copy(
            src_ref=attn_in.at[:, :, :, pl.ds(pl.multiple_of(peer * width, width), width)],
            dst_ref=got_attn.at[source],
            send_sem=attn_send.at[i],
            recv_sem=attn_recv.at[i],
            device_id={"head": peer},
            device_id_type=MESH,
        )

    def mlp_copy(i, peer, source):
        return pltpu.make_async_remote_copy(
            src_ref=mlp_in.at[:, :, pl.ds(pl.multiple_of(peer * units, units), units)],
            dst_ref=got_mlp.at[source],
            send_sem=mlp_send.at[i],
            recv_sem=mlp_recv.at[i],
            device_id={"head": peer},
            device_id_type=MESH,
        )

    def send_attn(i, _):
        attn_copy(i, peer_of(i), head).start()
        return 0

    def send_mlp(i, _):
        mlp_copy(i, peer_of(i), head).start()
        return 0

    def ring_copy(stream_, direction, step, slot):
        return pltpu.make_async_remote_copy(
            src_ref=weights.at[slot],
            dst_ref=weights.at[slot],
            send_sem=ring_send.at[stream_, direction, step],
            recv_sem=ring_recv.at[stream_, direction, step],
            device_id={"tile": up if direction == 0 else down},
            device_id_type=MESH,
        )

    def side_copy(index, slot, to):
        return pltpu.make_async_remote_copy(
            src_ref=weights.at[slot],
            dst_ref=weights.at[slot],
            send_sem=side_send.at[index],
            recv_sem=side_recv.at[index],
            device_id={"tile": to},
            device_id_type=MESH,
        )

    far, near = z_n // 2, z_n - 1 - z_n // 2
    reach = ((far, near), (near, far))

    def half_of(stream_):
        return half if stream_ == 0 else 1 - half

    def arrival(stream_, direction, step):
        offset = z_n - step if direction == 0 else step
        slot = shard_at(half_of(stream_), (depth + offset) % z_n, core)
        return slot, stream_ * z_n + (offset if offset < z_n else 0)

    def begin(stream_):
        slot = shard_at(half_of(stream_), depth, core)
        ring_copy(stream_, 0, 1, slot).start()
        ring_copy(stream_, 1, 1, slot).start()
        side_copy(stream_ * z_n, slot, sibling).start()

    def advance(stream_, step):
        for direction in (0, 1):
            if step <= reach[stream_][direction]:
                slot, number = arrival(stream_, direction, step)
                ring_copy(stream_, direction, step, slot).wait_recv()
                if step < reach[stream_][direction]:
                    ring_copy(stream_, direction, step + 1, slot).start()
                side_copy(number, slot, sibling).start()

    cross = 2 * z_n
    locals_ = local_copies()
    locals_[2].wait()
    locals_[3].wait()
    side_copy(cross, own_shard, across).start()
    begin(0)
    lax.fori_loop(1, heads_n, send_attn, 0)
    lax.fori_loop(1, heads_n, send_mlp, 0)

    even = lax.broadcasted_iota(jnp.int32, (own_slots, HEAD_DIM), 1) % 2 == 0
    even8 = even[:8]
    for j, gain_ref in enumerate((q_gain, k_gain)):
        gain = jnp.broadcast_to(gain_ref[...], (8, HEAD_DIM))
        swapped = swap_pairs(gain, even8)[0:1]
        table_c[j] = cosine[...] * gain_ref[...]
        table_s[j] = sine[...] * swapped

    def prepare(group):
        for block in range(3):
            where = pl.ds(pl.multiple_of(group * own_rows + block * own_slots, 8), own_slots)
            for j, target in enumerate((queries, keys)):
                raw = got_attn[group, block, j].astype(F32)
                for n in range(local_heads):
                    x = raw[:, n * HEAD_DIM : (n + 1) * HEAD_DIM]
                    r = lax.rsqrt(jnp.mean(x * x, axis=-1, keepdims=True) + 1e-06)
                    y = r * (x * table_c[j, where] + swap_pairs(x, even) * table_s[j, where])
                    target[n, where] = y
            raw = got_attn[group, block, 2].astype(F32)
            for n in range(local_heads):
                values[n, where] = raw[:, n * HEAD_DIM : (n + 1) * HEAD_DIM]

    def receive_attn(i, _):
        source = source_of(i)
        attn_copy(i, head, source).wait_recv()
        prepare(source)
        return 0

    def activate(group):
        for block in range(3):
            where = pl.ds(pl.multiple_of(group * own_rows + block * own_slots, 8), own_slots)
            x = got_mlp[group, block].astype(F32)
            inner = math.sqrt(2.0 / math.pi) * (x + 0.044715 * (x * x * x))
            mlp_act[where] = 0.5 * x * (1.0 + jnp.tanh(inner))

    def receive_mlp(i, _):
        source = source_of(i)
        mlp_copy(i, head, source).wait_recv()
        activate(source)
        return 0

    live = slot_number[...] < text_len[0]
    factor = math.log2(math.e) / math.sqrt(HEAD_DIM)
    band = rows // 3

    def attend(n):
        k = keys[n].astype(BF16)
        v = values[n].astype(BF16)
        for part in range(3):
            q = queries[n, pl.ds(part * band, band)].astype(BF16)
            scores = lax.dot_general(q, k, (((1,), (1,)), ((), ())), preferred_element_type=F32)
            scores = jnp.where(live, scores, -1e30)
            top = jnp.max(scores, axis=-1, keepdims=True)
            weight = jnp.exp2((scores - top) * factor)
            total = jnp.sum(weight, axis=-1, keepdims=True)
            mixed = jnp.dot(weight.astype(BF16), v, preferred_element_type=F32)
            act[pl.ds(part * band, band), n * HEAD_DIM : (n + 1) * HEAD_DIM] = (mixed / total).astype(BF16)

    locals_[0].wait()
    prepare(head)
    side_copy(cross, shard_at(1 - half, depth, core), across).wait_recv()
    begin(1)
    advance(0, 1)
    advance(1, 1)
    lax.fori_loop(1, heads_n // 2, receive_attn, 0)
    lax.fori_loop(heads_n // 2, heads_n, receive_attn, 0)
    advance(0, 2)
    advance(1, 2)
    for n in range(local_heads):
        attend(n)
    locals_[1].wait()
    activate(head)
    lax.fori_loop(1, heads_n, receive_mlp, 0)
    act[:, width:] = mlp_act[...].astype(BF16)
    locals_[4].wait()
    locals_[5].wait()

    def wait_sibling(offsets):
        for stream_ in (0, 1):
            for offset in offsets:
                slot = shard_at(half_of(stream_), (depth + offset) % z_n, 1 - core)
                side_copy(stream_ * z_n + offset, slot, sibling).wait_recv()

    def first_of(p, y):
        odd = (p + core) % 2
        return (1 - odd) * (y + 1 - 2 * (y % 2)) + odd * (y_n - 1 - y)

    def y_copy(p):
        return pltpu.make_async_remote_copy(
            src_ref=y_out.at[p],
            dst_ref=y_in.at[p],
            send_sem=y_send.at[p],
            recv_sem=y_recv.at[p],
            device_id={"head": first_of(p, row_y) * 2 + side_x},
            device_id_type=MESH,
        )

    def y_low_copy(p):
        return pltpu.make_async_remote_copy(
            src_ref=y_low.at[p],
            dst_ref=y_sum.at[p],
            send_sem=y_low_send.at[p],
            recv_sem=y_low_recv.at[p],
            device_id={"head": first_of(p + 1, row_y) * 2 + side_x},
            device_id_type=MESH,
        )

    def y_pass_copy(p):
        return pltpu.make_async_remote_copy(
            src_ref=y_pass.at[p],
            dst_ref=y_got.at[p],
            send_sem=y_pass_send.at[p],
            recv_sem=y_pass_recv.at[p],
            device_id={"head": head_at(0, 1)},
            device_id_type=MESH,
        )

    def x_copy(p):
        return pltpu.make_async_remote_copy(
            src_ref=x_out.at[p],
            dst_ref=x_in.at[p],
            send_sem=x_send.at[p],
            recv_sem=x_recv.at[p],
            device_id={"head": head_at(0, 1)},
            device_id_type=MESH,
        )

    def x_pass_copy(p, dy):
        return pltpu.make_async_remote_copy(
            src_ref=x_pass.at[p, dy],
            dst_ref=x_got.at[p, dy],
            send_sem=x_pass_send.at[p, dy],
            recv_sem=x_pass_recv.at[p, dy],
            device_id={"head": head_at(dy, 0)},
            device_id_type=MESH,
        )

    def group_rows(kind, p, group):
        return product[kind, p, pl.ds(pl.multiple_of(group * own_rows, 8), own_rows)]

    def offset_of(kind, p):
        return p + 1 if kind == 1 else (z_n - p) % z_n

    def y_second(p):
        y_copy(p).wait_recv()
        other = first_of(p + 1, row_y)
        for side in (0, 1):
            total = group_rows(0, p, other * 2 + side) + y_in[p, 1, side].astype(F32)
            y_low[p, side] = total.astype(BF16)
        y_low_copy(p).start()

    def y_third(p):
        y_low_copy(p).wait_recv()
        for dx in (0, 1):
            side = (side_x + dx) % 2
            total = group_rows(0, p, row_y * 2 + side)
            total = total + y_in[p, 0, side].astype(F32) + y_sum[p, side].astype(F32)
            if dx == 0:
                mine[0, p] = total
            else:
                y_pass[p] = total.astype(BF16)
        y_pass_copy(p).start()

    def x_second(p):
        x_copy(p).wait_recv()
        for dy in range(1, y_n):
            peer_y = (row_y + dy) % y_n
            total = group_rows(1, p, peer_y * 2 + side_x) + x_in[p, peer_y].astype(F32)
            x_pass[p, dy] = total.astype(BF16)
            x_pass_copy(p, dy).start()
        mine[1, p] = group_rows(1, p, head) + x_in[p, row_y].astype(F32)

    wait_sibling([offset_of(kind, 0) for kind in (0, 1)])

    def project(k, _):
        p, kind = k // 2, 1 - k % 2

        @pl.when(k == 2)
        def _():
            wait_sibling([offset_of(kind, 1) for kind in (0, 1)])
            for step in range(3, far):
                advance(0, step)
                advance(1, step)

        @pl.when(k == 4)
        def _():
            wait_sibling([offset_of(kind, p) for p in range(2, pairs - 1) for kind in (0, 1)])

        @pl.when(k == 2 * pairs - 2)
        def _():
            y_second(0)
            advance(0, far)
            advance(1, far)
            wait_sibling([offset_of(kind, pairs - 1) for kind in (0, 1)])

        offset = kind * (p + 1) + (1 - kind) * ((z_n - p) % z_n)
        nearest = (depth + offset) % z_n
        block = weights[pl.ds(nearest * 4, 4)].reshape(columns, width + units)
        product[kind, p] = lax.dot_general(
            act[...], block, (((1,), (1,)), ((), ())), preferred_element_type=F32
        )

        @pl.when(kind == 0)
        def _():
            peer_y = first_of(p, row_y)
            for place, target in enumerate((peer_y, first_of(p + 1, peer_y))):
                for side in (0, 1):
                    y_out[p, place, side] = group_rows(0, p, target * 2 + side).astype(BF16)
            y_copy(p).start()

        @pl.when(kind == 1)
        def _():
            for peer_y in range(y_n):
                x_out[p, peer_y] = group_rows(1, p, peer_y * 2 + 1 - side_x).astype(BF16)
            x_copy(p).start()

        return 0

    lax.fori_loop(0, 2 * pairs, project, 0)

    def collect(p):
        y_pass_copy(p).wait_recv()
        mine[0, p] = mine[0, p] + y_got[p].astype(F32)
        total = mine[1, p]
        for dy in range(1, y_n):
            x_pass_copy(p, dy).wait_recv()
            total = total + x_got[p, dy].astype(F32)
        mine[1, p] = total

    x_second(0)
    y_second(1)
    y_third(0)
    y_second(2)
    x_second(1)
    y_third(1)
    y_second(3)
    x_second(2)
    y_third(2)
    y_third(3)
    x_second(3)
    collect(0)
    collect(1)
    collect(2)
    collect(3)

    def sum_at(z):
        offset = (z + z_n - depth) % z_n
        kind = (offset + z_n - 1) % z_n // pairs
        p = (1 - kind) * (offset - 1) + kind * ((z_n - offset) % z_n)
        return mine[1 - kind, p]

    narrow = columns // 2
    for pair in range(z_n // 2):
        low, high = sum_at(2 * pair), sum_at(2 * pair + 1)
        for side in (0, 1):
            piece = slice(side * narrow, (side + 1) * narrow)
            total = jnp.concatenate([low[:, piece], high[:, piece]], axis=-1)
            start = side * narrow * z_n + pair * columns
            at = slice(start, start + columns)
            for block in range(3):
                part = slice(block * own_slots, (block + 1) * own_slots)
                new = stream[block, :, at].astype(F32) + gate[:, at] * (total[part] + bias_out[:, at])
                updated[block, :, at] = new
                hidden_out[block, :, at] = new.astype(BF16)

    for block in (1, 2):
        image = updated[block]
        center = image - jnp.mean(image, axis=-1, keepdims=True)
        variance = jnp.mean(center * center, axis=-1, keepdims=True)
        normed = center * lax.rsqrt(variance + 1e-06)
        modulated = ((1.0 + scale[...]) * normed + shift[...]).astype(BF16)
        velocity = lax.dot_general(
            modulated, final_w[...], (((1,), (1,)), ((), ())), preferred_element_type=F32
        )
        latent_out[block - 1] = latent[block - 1] + step_size[0] * (velocity + b_final[...])

    def drain(i, _):
        attn_copy(i, peer_of(i), head).wait_send()
        mlp_copy(i, peer_of(i), head).wait_send()
        return 0

    lax.fori_loop(1, heads_n, drain, 0)

    def drain_parts(p, _):
        for dy in range(1, y_n):
            x_pass_copy(p, dy).wait_send()
        y_copy(p).wait_send()
        y_low_copy(p).wait_send()
        y_pass_copy(p).wait_send()
        x_copy(p).wait_send()
        return 0

    lax.fori_loop(0, pairs, drain_parts, 0)
    side_copy(cross, own_shard, across).wait_send()
    for stream_ in (0, 1):
        for offset in range(z_n):
            slot = shard_at(half_of(stream_), (depth + offset) % z_n, core)
            side_copy(stream_ * z_n + offset, slot, sibling).wait_send()
        for direction in (0, 1):
            for step in range(1, reach[stream_][direction] + 1):
                offset = z_n - step + 1 if direction == 0 else step - 1
                slot = shard_at(half_of(stream_), (depth + offset) % z_n, core)
                ring_copy(stream_, direction, step, slot).wait_send()


def hand_on(hidden_in, latent_in, hidden_out, latent_out, sem):
    copies = (
        pltpu.make_async_copy(hidden_in, hidden_out, sem.at[0]),
        pltpu.make_async_copy(latent_in, latent_out, sem.at[1]),
    )
    for copy in copies:
        copy.start()
    for copy in copies:
        copy.wait()


def solution(mesh):
    heads_n = mesh.shape["head"]
    tiles_n = mesh.shape["tile"]
    z_n = tiles_n // 4
    pairs = 4
    cosine, sine, slot_number = rope_constants(heads_n)

    def per_device(
        attn_proj,
        mlp_proj,
        stream,
        text_len,
        q_gain,
        k_gain,
        w_out_attn,
        w_out_mlp,
        bias_out,
        gate_mod,
        final_shift,
        final_scale,
        w_final,
        b_final,
        latent,
        step_size,
    ):
        own_slots = attn_proj.shape[2]
        own_rows = 3 * own_slots
        rows = heads_n * own_rows
        features = attn_proj.shape[4]
        width, shard = w_out_attn.shape
        units = w_out_mlp.shape[0]
        local_heads = width // HEAD_DIM
        columns = features // (2 * pairs)
        y_n = heads_n // 2
        channels = w_final.shape[1]
        cfg = (heads_n, z_n, pairs, own_rows, own_slots)
        any_ = pl.BlockSpec(memory_space=pl.ANY)
        vmem = pl.BlockSpec(memory_space=pltpu.VMEM)
        smem = pl.BlockSpec(memory_space=pltpu.SMEM)
        dma = pltpu.SemaphoreType.DMA
        hidden, latent_next = pl.pallas_call(
            functools.partial(layer_kernel, cfg),
            out_shape=(
                jax.ShapeDtypeStruct((3, own_slots, features), BF16),
                jax.ShapeDtypeStruct((2, own_slots, channels), F32),
            ),
            in_specs=[smem, smem] + [any_] * 6 + [vmem] * 11,
            out_specs=(vmem, vmem),
            scratch_shapes=[
                pltpu.VMEM((heads_n, 3, 3, own_slots, width), BF16),
                pltpu.VMEM((heads_n, 3, own_slots, units), BF16),
                pltpu.VMEM((tiles_n, shard, width + units), BF16),
                pltpu.VMEM((local_heads, rows, HEAD_DIM), F32),
                pltpu.VMEM((local_heads, rows, HEAD_DIM), F32),
                pltpu.VMEM((local_heads, rows, HEAD_DIM), F32),
                pltpu.VMEM((rows, units), F32),
                pltpu.VMEM((rows, width + units), BF16),
                pltpu.VMEM((2, pairs, rows, columns), F32),
                pltpu.VMEM((pairs, 2, 2, own_rows, columns), BF16),
                pltpu.VMEM((pairs, 2, 2, own_rows, columns), BF16),
                pltpu.VMEM((pairs, 2, own_rows, columns), BF16),
                pltpu.VMEM((pairs, 2, own_rows, columns), BF16),
                pltpu.VMEM((pairs, own_rows, columns), BF16),
                pltpu.VMEM((pairs, own_rows, columns), BF16),
                pltpu.VMEM((pairs, y_n, own_rows, columns), BF16),
                pltpu.VMEM((pairs, y_n, own_rows, columns), BF16),
                pltpu.VMEM((pairs, y_n, own_rows, columns), BF16),
                pltpu.VMEM((pairs, y_n, own_rows, columns), BF16),
                pltpu.VMEM((2, pairs, own_rows, columns), F32),
                pltpu.VMEM((3, own_slots, features), F32),
                pltpu.VMEM((3, own_slots, features), BF16),
                pltpu.VMEM((channels, features), BF16),
                pltpu.VMEM((2, rows, HEAD_DIM), F32),
                pltpu.VMEM((2, rows, HEAD_DIM), F32),
                dma((6,)),
                dma((heads_n,)),
                dma((heads_n,)),
                dma((heads_n,)),
                dma((heads_n,)),
                dma((2, 2, z_n)),
                dma((2, 2, z_n)),
                dma((2 * z_n + 1,)),
                dma((2 * z_n + 1,)),
                dma((pairs,)),
                dma((pairs,)),
                dma((pairs,)),
                dma((pairs,)),
                dma((pairs,)),
                dma((pairs,)),
                dma((pairs,)),
                dma((pairs,)),
                dma((pairs, y_n)),
                dma((pairs, y_n)),
            ],
            compiler_params=pltpu.CompilerParams(
                collective_id=0, has_side_effects=True, vmem_limit_bytes=56 * 1024 * 1024
            ),
        )(
            text_len,
            step_size,
            jnp.transpose(attn_proj[0], (0, 2, 1, 3)),
            mlp_proj[0],
            stream[0],
            w_out_attn.T,
            w_out_mlp.T,
            w_final.T,
            jnp.asarray(cosine.reshape(rows, HEAD_DIM)),
            jnp.asarray(sine.reshape(rows, HEAD_DIM)),
            jnp.asarray(slot_number),
            q_gain[None],
            k_gain[None],
            bias_out[None],
            gate_mod,
            final_shift,
            final_scale,
            b_final[None],
            latent[0],
        )
        hidden, latent_next = pl.pallas_call(
            hand_on,
            out_shape=(
                jax.ShapeDtypeStruct(hidden.shape, hidden.dtype),
                jax.ShapeDtypeStruct(latent_next.shape, latent_next.dtype),
            ),
            in_specs=[vmem, vmem],
            out_specs=(any_, any_),
            scratch_shapes=[dma((2,))],
        )(hidden, latent_next)
        return hidden[None], latent_next[None]

    placed = (
        P("tile", None, "head", None, None),
        P("tile", None, "head", None),
        P("tile", None, "head", None),
        P("tile"),
        P(),
        P(),
        P("head", "tile"),
        P("head", "tile"),
        P(),
        P("tile", None),
        P("tile", None),
        P("tile", None),
        P(),
        P(),
        P("tile", None, "head", None),
        P("tile"),
    )
    return jax.shard_map(
        per_device,
        mesh=mesh,
        in_specs=placed,
        out_specs=(P("tile", None, "head", None), P("tile", None, "head", None)),
        check_vma=False,
    )
```
